32 devices in a mesh: dp: 8 (over z, y), fsdp: 4 (over x, core).
Axes of the slice: x: 2, y: 2, z: 4, core: 2. Of those that a mesh axis runs over, the one named last changes fastest.
Arguments:
- keys: bfloat16 [256, 8, 896], P(('dp', 'fsdp')), may hold values from -8 to 8
- residual: bfloat16 [256, 8, 896], P(('dp', 'fsdp')), may hold values from -6 to 6
- se_reduce: bfloat16 [896, 224], P('fsdp'), may hold values from -0.625 to 0.625
- se_expand: bfloat16 [896, 224], P('fsdp'), may hold values from -1.25 to 1.25
- conv_weight: bfloat16 [3, 896, 896], P(None, 'fsdp'), may hold values from -0.1875 to 0.1875
- bn_gain: float32 [896], replicated, may hold values from 0.1 to 1.9
- bn_bias: float32 [896], replicated, may hold values from -3 to 3
- shuffle: int32 [256], P(('dp', 'fsdp')), may hold values from 0 to 63, as said below
- unshuffle: int32 [256], P(('dp', 'fsdp')), may hold values from 0 to 63, as said below
Outputs:
- encoded: bfloat16 [256, 8, 896], P(('dp', 'fsdp'))
The draws below stay inside these ranges and needn't reach their ends.
Inputs may be any that keep to these rules, and one draw needn't show every extreme that they name: `shuffle`: A permutation of the 64 positions within each group of devices sharing an fsdp index (positions ordered by dp index, then by image); each device sends exactly 1 of its images to every device of its group. `unshuffle`: the inverse of shuffle within each group.
All inputs are finite; a program needn't handle non-finite values.
Results may differ from the reference program's by a relative error of at most 0.013.
Values may be sent and summed in bfloat16 or wider, within the bound.
A program may use at most 64 MiB of HBM per device.

```python
import jax
import jax.numpy as jnp
from jax import lax

C = 896
S = 224
PIX = 8
LAYERS = 3
PER_PEER = 1
IMG_DEV = 8
BATCH = 256
N_DP = 8
N_FSDP = 4


def balanced_positions(key):
    first_key, second_key = jax.random.split(jax.random.fold_in(key, 7101))
    source_perm = jax.vmap(lambda one_key: jax.random.permutation(one_key, IMG_DEV))(jax.random.split(first_key, N_FSDP * N_DP))
    source_perm = source_perm.reshape(N_FSDP, N_DP, IMG_DEV).astype(jnp.int32)
    slot_perm = jax.vmap(lambda one_key: jax.random.permutation(one_key, IMG_DEV))(jax.random.split(second_key, N_FSDP * N_DP))
    slot_perm = slot_perm.reshape(N_FSDP, N_DP, IMG_DEV).astype(jnp.int32)
    target_device = source_perm // PER_PEER
    within_peer = source_perm % PER_PEER
    source_index = jnp.arange(N_DP, dtype=jnp.int32)[None, :, None]
    incoming = source_index * PER_PEER + within_peer
    fsdp_index = jnp.arange(N_FSDP, dtype=jnp.int32)[:, None, None]
    positions = target_device * IMG_DEV + slot_perm[fsdp_index, target_device, incoming]
    own_position = source_index * IMG_DEV + jnp.arange(IMG_DEV, dtype=jnp.int32)[None, None, :]
    fsdp_full = jnp.broadcast_to(fsdp_index, positions.shape)
    inverse = jnp.zeros((N_FSDP, N_DP * IMG_DEV), jnp.int32).at[fsdp_full, positions].set(jnp.broadcast_to(own_position, positions.shape))
    inverse = inverse.reshape(N_FSDP, N_DP, IMG_DEV)
    shuffle_flat = jnp.transpose(positions, (1, 0, 2)).reshape(BATCH)
    inverse_flat = jnp.transpose(inverse, (1, 0, 2)).reshape(BATCH)
    return (shuffle_flat, inverse_flat)


def draw_shuffle(key, part):
    return balanced_positions(key)[0]


def draw_unshuffle(key, part):
    return balanced_positions(key)[1]


def draw_keys(key, part):
    noise_key, scale_key = jax.random.split(jax.random.fold_in(key, 3301), 2)
    image_scale = jnp.exp(jax.random.uniform(scale_key, (BATCH, 1, 1), jnp.float32, jnp.log(0.3), jnp.log(3.0)))
    base = jax.random.normal(noise_key, (BATCH, PIX, C), jnp.float32)
    return jnp.clip(base * image_scale, -8.0, 8.0).astype(jnp.bfloat16)


def block_scale(stream_key, dims, pieces, least, largest):
    factor_of, own = 1.0, jax.random.fold_in(stream_key, 6)
    for position, parts in pieces:
        draws = jnp.exp(jax.random.uniform(jax.random.fold_in(own, position), (parts,), jnp.float32, least / len(pieces), largest / len(pieces)))
        factor_of = factor_of * jnp.repeat(draws, dims[position] // parts).reshape([-1 if axis == position else 1 for axis in range(len(dims))])
    return factor_of


def noise(key, dims, width, reach, cuts=(), held_as=jnp.bfloat16):
    values = width * jax.random.normal(key, dims, jnp.float32)
    if cuts:
        values = values * block_scale(key, dims, cuts, -0.22, 0.18)
    return jnp.clip(values, -reach, reach).astype(held_as)


def setup_inputs(seed: int = 0) -> dict:
    key_of = jax.random.split(jax.random.key(seed), 10)
    return {
        "keys": draw_keys(jax.random.fold_in(key_of[9], 71), 0),
        "residual": noise(key_of[1], (BATCH, PIX, C), 1.0, 6.0, ((0, 32),)),
        "se_reduce": noise(key_of[2], (C, S), (C // 9) ** -0.5, 0.625, ((0, 4),)),
        "se_expand": noise(key_of[3], (C, S), (S // 9) ** -0.5, 1.25, ((0, 4),)),
        "conv_weight": noise(key_of[4], (LAYERS, C, C), C ** -0.5, 0.1875, ((1, 4),)),
        "bn_gain": jnp.clip(1.0 + 0.18 * jax.random.normal(key_of[5], (C,), jnp.float32), 0.1, 1.9),
        "bn_bias": noise(key_of[6], (C,), 0.5, 3.0, (), jnp.float32),
        "shuffle": draw_shuffle(jax.random.fold_in(key_of[9], 71), 0),
        "unshuffle": draw_unshuffle(jax.random.fold_in(key_of[9], 71), 0),
    }


epsilon = 1e-05

def encode_block(batch_block, se_reduce, se_expand, conv_weight):
    images, positions, channels = batch_block.shape
    entry = batch_block.reshape(images * positions, channels)
    for layer in range(LAYERS - 1):
        entry = jax.nn.relu(jnp.dot(entry, conv_weight[layer], preferred_element_type=jnp.float32)).astype(jnp.bfloat16)
    entry = entry.reshape(images, positions, channels)
    pooled = lax.optimization_barrier(jnp.mean(entry, axis=1, dtype=jnp.float32)).astype(jnp.bfloat16)
    squeeze_act = jax.nn.relu(jnp.dot(pooled, se_reduce, preferred_element_type=jnp.float32)).astype(jnp.bfloat16)
    excite = jax.nn.sigmoid(jnp.dot(squeeze_act, se_expand.T, preferred_element_type=jnp.float32))
    scaled = (entry * excite[:, None, :]).astype(jnp.bfloat16)
    flat = scaled.reshape(-1, channels)
    projected = jnp.dot(flat, conv_weight[LAYERS - 1], preferred_element_type=jnp.float32)
    return projected.reshape(batch_block.shape)

def reference(keys, residual, se_reduce, se_expand, conv_weight, bn_gain, bn_bias, shuffle, unshuffle):
    channels = keys.shape[2]
    blocks = keys.reshape(N_DP, N_FSDP * IMG_DEV, PIX, channels)
    projected = lax.map(lambda part_block: encode_block(part_block, se_reduce, se_expand, conv_weight), blocks)
    projected = projected.reshape(N_DP, N_FSDP, IMG_DEV, PIX, channels)
    row_sums = lax.optimization_barrier(jnp.sum(projected, axis=3))
    square_sums = lax.optimization_barrier(jnp.sum(projected * projected, axis=3))

    def grouped(table):
        return jnp.transpose(table, (1, 0, 2, 3)).reshape(N_FSDP, N_DP * IMG_DEV, channels)
    anchor = jnp.transpose(unshuffle.reshape(N_DP, N_FSDP, IMG_DEV), (1, 0, 2)).reshape(N_FSDP, N_DP * IMG_DEV)
    anchor = anchor.astype(jnp.int32)
    sum_shuffled = jnp.take_along_axis(grouped(row_sums), anchor[:, :, None], axis=1)
    square_shuffled = jnp.take_along_axis(grouped(square_sums), anchor[:, :, None], axis=1)
    sum_device = lax.optimization_barrier(jnp.sum(sum_shuffled.reshape(N_FSDP, N_DP, IMG_DEV, channels), axis=2))
    square_device = lax.optimization_barrier(jnp.sum(square_shuffled.reshape(N_FSDP, N_DP, IMG_DEV, channels), axis=2))
    count = IMG_DEV * PIX
    mean_bn = sum_device / count
    var_bn = square_device / count - mean_bn * mean_bn
    inv_std = lax.rsqrt(var_bn + epsilon)
    target_device = (shuffle.reshape(N_DP, N_FSDP, IMG_DEV) // IMG_DEV).astype(jnp.int32)
    fsdp_index = jnp.arange(N_FSDP, dtype=jnp.int32)[None, :, None]
    mean_image = mean_bn[fsdp_index, target_device]
    scale_image = inv_std[fsdp_index, target_device] * bn_gain
    normed = ((projected - mean_image[:, :, :, None, :]) * scale_image[:, :, :, None, :] + bn_bias).astype(jnp.bfloat16)
    normed = lax.optimization_barrier(normed)
    normed = normed.reshape(keys.shape)
    encoded = jax.nn.relu(normed.astype(jnp.float32) + residual.astype(jnp.float32))
    return encoded.astype(jnp.bfloat16)
```

```python
import functools

import jax
import jax.numpy as jnp
from jax import lax
from jax.experimental import pallas as pl
from jax.experimental.pallas import tpu as pltpu
from jax.sharding import PartitionSpec as P

epsilon = 1e-05
lane = 128
MESH = pl.DeviceIdType.MESH


def project_rows(flat, weight_rows):
    return jnp.dot(
        flat,
        lax.all_gather(weight_rows, "fsdp", axis=0, tiled=True),
        preferred_element_type=jnp.float32,
    )


def reorder(images_block, order):
    images, positions, channels = images_block.shape
    chosen = (order[:, None] == jnp.arange(images)[None, :]).astype(images_block.dtype)
    picked = jnp.dot(
        chosen,
        images_block.reshape(images, positions * channels),
        preferred_element_type=jnp.float32,
    )
    return picked.astype(images_block.dtype).reshape(images_block.shape)


def encode_block(batch_block, reduce_full, expand_full, conv_weight):
    images, positions, channels = batch_block.shape
    layers = conv_weight.shape[0]
    flat = batch_block.reshape(images * positions, channels)
    for layer in range(layers - 1):
        flat = jax.nn.relu(project_rows(flat, conv_weight[layer])).astype(jnp.bfloat16)
    entry = flat.reshape(images, positions, channels)
    pooled = jnp.mean(entry, axis=1, dtype=jnp.float32).astype(jnp.bfloat16)
    squeeze_act = jax.nn.relu(
        jnp.dot(pooled, reduce_full, preferred_element_type=jnp.float32)
    ).astype(jnp.bfloat16)
    excite = jax.nn.sigmoid(
        lax.dot_general(
            squeeze_act, expand_full, (((1,), (1,)), ((), ())), preferred_element_type=jnp.float32
        )
    )
    scaled = (entry * excite[:, None, :]).astype(jnp.bfloat16).reshape(images * positions, channels)
    projected = project_rows(scaled, conv_weight[layers - 1])
    return projected.reshape(images, positions, channels)


def local_general(keys, residual, se_reduce, se_expand, conv_weight, bn_gain, bn_bias, shuffle, unshuffle):
    images, positions, channels = keys.shape
    count = images * positions
    reduce_full, expand_full = (
        lax.all_gather(se_reduce, "fsdp", axis=0, tiled=True),
        lax.all_gather(se_expand, "fsdp", axis=0, tiled=True),
    )
    send_order = jnp.argsort(shuffle)
    back_order = jnp.argsort(send_order)
    outgoing = reorder(keys, send_order)
    arrived = lax.all_to_all(outgoing, "dp", split_axis=0, concat_axis=0, tiled=True)
    projected = encode_block(arrived, reduce_full, expand_full, conv_weight)
    row_sums = jnp.sum(projected, axis=(0, 1))
    square_sums = jnp.sum(projected * projected, axis=(0, 1))
    mean_rows = row_sums / count
    variance = square_sums / count - mean_rows * mean_rows
    scale_rows = lax.rsqrt(variance + epsilon) * bn_gain
    normed_here = ((projected - mean_rows) * scale_rows + bn_bias).astype(jnp.bfloat16)
    returned = lax.all_to_all(normed_here, "dp", split_axis=0, concat_axis=0, tiled=True)
    normed = reorder(returned, back_order)
    encoded = jax.nn.relu(normed.astype(jnp.float32) + residual.astype(jnp.float32))
    return encoded.astype(jnp.bfloat16)


def fused_kernel(
    n_dp,
    images,
    positions,
    keys_ref,
    reduce_ref,
    expand_ref,
    weight_ref,
    gain_ref,
    bias_ref,
    shuffle_ref,
    out_ref,
    w,
    red,
    exp,
    kbuf,
    psend,
    precv,
    se_send,
    se_recv,
    last_send,
    last_recv,
    keysv,
    ksend,
    nsend,
    nrecv,
    key_sem,
    key_send_sem,
    key_recv_sem,
    weight_sem,
    layer_sem,
    se_sem,
    last_sem,
    back_send_sem,
    back_recv_sem,
    ready_sem,
):
    me = lax.axis_index("dp")
    f = lax.axis_index("fsdp")
    x, c = f // 2, f % 2
    sibling = 2 * x + (1 - c)
    peer = 2 * (1 - x) + c
    layers, rows_dev, channels = weight_ref.shape
    half = 2 * rows_dev
    window = kbuf.shape[3]
    pad = window - half
    rows = images * positions
    own_lo = pl.multiple_of(x * (channels - window), lane)
    peer_lo = pl.multiple_of((1 - x) * (channels - window), lane)
    base = pl.multiple_of(x * pad + c * rows_dev, 16)

    barrier = pltpu.get_barrier_semaphore()
    for k in range(n_dp):
        target = lax.rem(me + k, n_dp)
        for column in (f, peer):
            if k > 0 or column is peer:
                pl.semaphore_signal(
                    barrier,
                    inc=1,
                    device_id={"dp": target, "fsdp": column},
                    device_id_type=MESH,
                )

    @pl.when(c == 0)
    def _():
        pl.semaphore_signal(barrier, inc=1, device_id={"fsdp": sibling}, device_id_type=MESH)

    keys_local = pltpu.make_async_copy(keys_ref, keysv, key_sem)
    keys_local.start()
    sources = [weight_ref.at[l] for l in range(layers)] + [reduce_ref, expand_ref]
    targets = [w.at[l] for l in range(layers)] + [red, exp]
    local_copies = []
    for s, (src, dst) in enumerate(zip(sources, targets)):
        copy = pltpu.make_async_copy(src, dst.at[pl.ds(base, rows_dev), :], weight_sem.at[0, s])
        copy.start()
        local_copies.append(copy)

    zero_lo = pl.multiple_of((1 - x) * half, 16)
    for l in range(layers):
        w[l, pl.ds(zero_lo, pad), :] = jnp.zeros((pad, channels), w.dtype)
    red[pl.ds(zero_lo, pad), :] = jnp.zeros((pad, red.shape[1]), red.dtype)
    exp[pl.ds(zero_lo, pad), :] = jnp.zeros((pad, exp.shape[1]), exp.dtype)

    dests = [lax.div(shuffle_ref[i], images) for i in range(images)]
    keys_local.wait()
    for e in range(n_dp):
        chosen = jnp.int32(0)
        for i in range(images):
            chosen = jnp.where(dests[i] == e, i, chosen)
        ksend[e] = keysv[chosen]

    pl.semaphore_wait(barrier, 2 * n_dp - 1 + c)

    @pl.when(c == 1)
    def _():
        pl.semaphore_signal(ready_sem, inc=1, device_id={"fsdp": sibling}, device_id_type=MESH)

    key_copies = []
    for k in range(n_dp):
        target = lax.rem(me + k, n_dp)
        for side, (column, lo) in enumerate(((f, own_lo), (peer, peer_lo))):
            src = ksend.at[target, :, pl.ds(lo, window)]
            dst = kbuf.at[x, me]
            if k == 0 and side == 0:
                copy = pltpu.make_async_copy(src, dst, key_recv_sem.at[side, k])
            else:
                copy = pltpu.make_async_remote_copy(
                    src_ref=src,
                    dst_ref=dst,
                    send_sem=key_send_sem.at[side, k],
                    recv_sem=key_recv_sem.at[side, k],
                    device_id={"dp": target, "fsdp": column},
                    device_id_type=MESH,
                )
            copy.start()
            key_copies.append(copy)

    @pl.when(c == 0)
    def _():
        pl.semaphore_wait(ready_sem, 1)

    shared = {}
    for s in (0, 1, layers, layers + 1, *range(2, layers)):
        shared[s] = pltpu.make_async_remote_copy(
            src_ref=sources[s],
            dst_ref=targets[s].at[pl.ds(base, rows_dev), :],
            send_sem=weight_sem.at[1, s],
            recv_sem=weight_sem.at[2, s],
            device_id={"fsdp": sibling},
            device_id_type=MESH,
        )
        shared[s].start()

    def have_weights(s):
        local_copies[s].wait()
        shared[s].wait_recv()

    pending = []

    def to_peer(src, dst, sems):
        copy = pltpu.make_async_remote_copy(
            src_ref=src,
            dst_ref=dst,
            send_sem=sems.at[0],
            recv_sem=sems.at[1],
            device_id={"fsdp": peer},
            device_id_type=MESH,
        )
        copy.start()
        pending.append(copy)
        return copy

    chunks = psend.shape[1]
    part_rows = rows // chunks
    part_images = 2 * images // chunks
    key_copies[0].wait()
    for copy in key_copies[1:]:
        copy.wait_recv()
    half_images = images // chunks
    entries = [
        kbuf[:, j * half_images : (j + 1) * half_images]
        .astype(jnp.float32)
        .reshape(2 * part_rows, window)
        .astype(jnp.bfloat16)
        for j in range(chunks)
    ]
    copies = [None] * chunks
    mines = [None] * chunks

    def settle(l, j):
        copies[j].wait_recv()
        full = mines[j] + precv[l, j].astype(jnp.float32)
        return jnp.maximum(full, 0.0).astype(jnp.bfloat16)

    def own_part(l, j):
        return jnp.dot(
            entries[j], w[l, :, pl.ds(own_lo, window)], preferred_element_type=jnp.float32
        )

    for l in range(layers - 1):
        have_weights(l)
        for j in range(chunks):
            if l > 0:
                entries[j] = settle(l - 1, j)
            theirs = jnp.dot(
                entries[j], w[l, :, pl.ds(peer_lo, window)], preferred_element_type=jnp.float32
            )
            psend[l, j] = theirs.astype(jnp.bfloat16)
            copies[j] = to_peer(psend.at[l, j], precv.at[l, j], layer_sem.at[l, j])
            if l > 0:
                mines[j] = own_part(l, j)
        if l == 0:
            mines = [own_part(l, j) for j in range(chunks)]

    have_weights(layers)
    have_weights(layers + 1)
    wides, parts = [None] * chunks, [None] * chunks
    for j in range(chunks):
        entry = settle(layers - 2, j)
        wides[j] = entry.astype(jnp.float32).reshape(part_images, positions, window)
        pooled = (jnp.sum(wides[j], axis=1) * (1.0 / positions)).astype(jnp.bfloat16)
        parts[j] = jnp.dot(pooled, red[...], preferred_element_type=jnp.float32)
        se_send[j] = parts[j]
        copies[j] = to_peer(se_send.at[j], se_recv.at[j], se_sem.at[j])

    have_weights(layers - 1)
    for j in range(chunks):
        copies[j].wait_recv()
        squeeze_act = jnp.maximum(parts[j] + se_recv[j], 0.0).astype(jnp.bfloat16)
        excite = jax.nn.sigmoid(
            lax.dot_general(
                squeeze_act, exp[...], (((1,), (1,)), ((), ())), preferred_element_type=jnp.float32
            )
        )
        scaled = (wides[j] * excite[:, None, :]).astype(jnp.bfloat16)
        both = jnp.dot(
            scaled.reshape(2 * part_rows, window), w[layers - 1], preferred_element_type=jnp.float32
        )
        low, high = both[:part_rows], both[part_rows:]
        last_send[j] = jnp.where(x == 0, high, low).astype(jnp.bfloat16)
        copies[j] = to_peer(last_send.at[j], last_recv.at[j], last_sem.at[j])
        mines[j] = jnp.where(x == 0, low, high)
    for j in range(chunks):
        copies[j].wait_recv()
        mines[j] = mines[j] + last_recv[j].astype(jnp.float32)
    count = images * positions
    mean_rows = sum(jnp.sum(mine, axis=0, keepdims=True) for mine in mines) / count
    squares = sum(jnp.sum(mine * mine, axis=0, keepdims=True) for mine in mines) / count
    scale_rows = lax.rsqrt(squares - mean_rows * mean_rows + epsilon) * gain_ref[...].reshape(
        1, channels
    )
    bias_rows = bias_ref[...].reshape(1, channels)
    for j in range(chunks):
        normed = (mines[j] - mean_rows) * scale_rows + bias_rows
        nsend[j * half_images : (j + 1) * half_images] = normed.reshape(
            half_images, positions, channels
        ).astype(jnp.bfloat16)

    back_copies = []
    for k in range(1, n_dp):
        target = lax.rem(me + k, n_dp)
        copy = pltpu.make_async_remote_copy(
            src_ref=nsend.at[target],
            dst_ref=nrecv.at[me],
            send_sem=back_send_sem.at[k - 1],
            recv_sem=back_recv_sem.at[k - 1],
            device_id={"dp": target},
            device_id_type=MESH,
        )
        copy.start()
        back_copies.append(copy)
    nrecv[me] = nsend[me]
    for copy in back_copies:
        copy.wait_recv()
    for i in range(images):
        out_ref[i] = nrecv[dests[i]]
    for copy in key_copies[1:] + list(shared.values()) + pending + back_copies:
        copy.wait_send()


def local_fused(n_dp, keys, residual, se_reduce, se_expand, conv_weight, bn_gain, bn_bias, shuffle, unshuffle):
    images, positions, channels = keys.shape
    layers, rows_dev, _ = conv_weight.shape
    units = se_reduce.shape[1]
    chunks = 4
    rows = images * positions
    half = 2 * rows_dev
    window = -(-half // lane) * lane
    bf16, f32 = jnp.bfloat16, jnp.float32
    vmem = pl.BlockSpec(memory_space=pltpu.VMEM)
    anywhere = pl.BlockSpec(memory_space=pl.ANY)
    dma = pltpu.SemaphoreType.DMA
    normed = pl.pallas_call(
        functools.partial(fused_kernel, n_dp, images, positions),
        out_shape=pltpu.VMEM((images, positions, channels), bf16),
        in_specs=[anywhere] * 4 + [vmem] * 2 + [pl.BlockSpec(memory_space=pltpu.SMEM)],
        out_specs=vmem,
        scratch_shapes=[
            pltpu.VMEM((layers, window, channels), bf16),
            pltpu.VMEM((window, units), bf16),
            pltpu.VMEM((window, units), bf16),
            pltpu.VMEM((2, images, positions, window), bf16),
            pltpu.VMEM((layers - 1, chunks, 2 * rows // chunks, window), bf16),
            pltpu.VMEM((layers - 1, chunks, 2 * rows // chunks, window), bf16),
            pltpu.VMEM((chunks, 2 * images // chunks, units), f32),
            pltpu.VMEM((chunks, 2 * images // chunks, units), f32),
            pltpu.VMEM((chunks, rows // chunks, channels), bf16),
            pltpu.VMEM((chunks, rows // chunks, channels), bf16),
            pltpu.VMEM((images, positions, channels), bf16),
            pltpu.VMEM((n_dp, positions, channels), bf16),
            pltpu.VMEM((images, positions, channels), bf16),
            pltpu.VMEM((n_dp, positions, channels), bf16),
            dma,
            dma((2, n_dp)),
            dma((2, n_dp)),
            dma((3, layers + 2)),
            dma((layers - 1, chunks, 2)),
            dma((chunks, 2)),
            dma((chunks, 2)),
            dma((n_dp - 1,)),
            dma((n_dp - 1,)),
            pltpu.SemaphoreType.REGULAR,
        ],
        compiler_params=pltpu.CompilerParams(collective_id=0, has_side_effects=True),
        name="fused_encoder",
    )(
        keys,
        se_reduce,
        se_expand,
        conv_weight,
        bn_gain,
        bn_bias,
        shuffle,
    )
    encoded = jax.nn.relu(normed.astype(f32) + residual.astype(f32))
    return encoded.astype(bf16)


def solution(mesh):
    placed = (
        P(("dp", "fsdp"), None, None),
        P(("dp", "fsdp"), None, None),
        P("fsdp", None),
        P("fsdp", None),
        P(None, "fsdp", None),
        P(),
        P(),
        P(("dp", "fsdp")),
        P(("dp", "fsdp")),
    )
    n_dp, n_fsdp = mesh.shape["dp"], mesh.shape["fsdp"]

    def local(keys, *others):
        if n_fsdp == 4 and keys.shape[0] == n_dp:
            return local_fused(n_dp, keys, *others)
        return local_general(keys, *others)

    return jax.shard_map(
        local, mesh=mesh, in_specs=placed, out_specs=P(("dp", "fsdp"), None, None), check_vma=False
    )
```

```python
import functools

import jax
import jax.numpy as jnp
from jax import lax
from jax.experimental import pallas as pl
from jax.experimental.pallas import tpu as pltpu
from jax.sharding import PartitionSpec as P

epsilon = 1e-05
lane = 128
MESH = pl.DeviceIdType.MESH


def project_rows(flat, weight_rows):
    return jnp.dot(
        flat,
        lax.all_gather(weight_rows, "fsdp", axis=0, tiled=True),
        preferred_element_type=jnp.float32,
    )


def reorder(images_block, order):
    images, positions, channels = images_block.shape
    chosen = (order[:, None] == jnp.arange(images)[None, :]).astype(images_block.dtype)
    picked = jnp.dot(
        chosen,
        images_block.reshape(images, positions * channels),
        preferred_element_type=jnp.float32,
    )
    return picked.astype(images_block.dtype).reshape(images_block.shape)


def encode_block(batch_block, reduce_full, expand_full, conv_weight):
    images, positions, channels = batch_block.shape
    layers = conv_weight.shape[0]
    flat = batch_block.reshape(images * positions, channels)
    for layer in range(layers - 1):
        flat = jax.nn.relu(project_rows(flat, conv_weight[layer])).astype(jnp.bfloat16)
    entry = flat.reshape(images, positions, channels)
    pooled = jnp.mean(entry, axis=1, dtype=jnp.float32).astype(jnp.bfloat16)
    squeeze_act = jax.nn.relu(
        jnp.dot(pooled, reduce_full, preferred_element_type=jnp.float32)
    ).astype(jnp.bfloat16)
    excite = jax.nn.sigmoid(
        lax.dot_general(
            squeeze_act, expand_full, (((1,), (1,)), ((), ())), preferred_element_type=jnp.float32
        )
    )
    scaled = (entry * excite[:, None, :]).astype(jnp.bfloat16).reshape(images * positions, channels)
    projected = project_rows(scaled, conv_weight[layers - 1])
    return projected.reshape(images, positions, channels)


def local_general(keys, residual, se_reduce, se_expand, conv_weight, bn_gain, bn_bias, shuffle, unshuffle):
    images, positions, channels = keys.shape
    count = images * positions
    reduce_full, expand_full = (
        lax.all_gather(se_reduce, "fsdp", axis=0, tiled=True),
        lax.all_gather(se_expand, "fsdp", axis=0, tiled=True),
    )
    send_order = jnp.argsort(shuffle)
    back_order = jnp.argsort(send_order)
    outgoing = reorder(keys, send_order)
    arrived = lax.all_to_all(outgoing, "dp", split_axis=0, concat_axis=0, tiled=True)
    projected = encode_block(arrived, reduce_full, expand_full, conv_weight)
    row_sums = jnp.sum(projected, axis=(0, 1))
    square_sums = jnp.sum(projected * projected, axis=(0, 1))
    mean_rows = row_sums / count
    variance = square_sums / count - mean_rows * mean_rows
    scale_rows = lax.rsqrt(variance + epsilon) * bn_gain
    normed_here = ((projected - mean_rows) * scale_rows + bn_bias).astype(jnp.bfloat16)
    returned = lax.all_to_all(normed_here, "dp", split_axis=0, concat_axis=0, tiled=True)
    normed = reorder(returned, back_order)
    encoded = jax.nn.relu(normed.astype(jnp.float32) + residual.astype(jnp.float32))
    return encoded.astype(jnp.bfloat16)


ORDER = (0, 1)


def fused_kernel(
    n_dp,
    images,
    positions,
    keys_ref,
    reduce_ref,
    expand_ref,
    weight_ref,
    gain_ref,
    bias_ref,
    shuffle_ref,
    out_ref,
    w,
    w_last,
    red,
    exp,
    relay_w,
    relay_red,
    relay_exp,
    kbuf,
    psend,
    precv,
    rsend,
    rrecv,
    keysv,
    ksend,
    nsend,
    nrecv,
    key_sem,
    key_send_sem,
    key_recv_sem,
    local_sem,
    pair_send_sem,
    pair_recv_sem,
    cross_send_sem,
    cross_recv_sem,
    spread_send_sem,
    spread_recv_sem,
    narrow_sem,
    wide_sem,
    back_send_sem,
    back_recv_sem,
):
    me = lax.axis_index("dp")
    f = lax.axis_index("fsdp")
    x, c = f // 2, f % 2
    hub = 2 * x + 1
    peer_hub = 2 * (1 - x) + 1
    peer_even = 2 * (1 - x)
    layers, rows_dev, channels = weight_ref.shape
    half = 2 * rows_dev
    window = kbuf.shape[4]
    pad = window - half
    rows = images * positions
    piece = half // 4
    quarter = lax.rem(me, 4)
    square = me - quarter
    own_lo = pl.multiple_of(x * (channels - window), lane)
    peer_lo = pl.multiple_of((1 - x) * (channels - window), lane)
    base = pl.multiple_of(x * pad + c * rows_dev, 16)
    last_base = pl.multiple_of(f * rows_dev, 16)

    barrier = pltpu.get_barrier_semaphore()

    def greet(dp, fsdp):
        pl.semaphore_signal(
            barrier, inc=1, device_id={"dp": dp, "fsdp": fsdp}, device_id_type=MESH
        )

    @pl.when(c == 1)
    def _():
        for k in range(n_dp):
            target = lax.rem(me + k, n_dp)
            greet(target, 2 * x)
            greet(target, 2 * (1 - x))
            greet(target, peer_hub)
            if k > 0:
                greet(target, hub)

    @pl.when(c == 0)
    def _():
        for k in range(n_dp):
            greet(lax.rem(me + k, n_dp), hub)
        greet(me, peer_even)
        greet(me, peer_hub)

    keys_local = pltpu.make_async_copy(keys_ref, keysv, key_sem)
    keys_local.start()

    own_sources = [weight_ref.at[0], weight_ref.at[1], reduce_ref, expand_ref, weight_ref.at[2]]
    full_targets = [w.at[0], w.at[1], red, exp, w_last]

    def shard_of(s):
        return full_targets[s].at[pl.ds(base if s < 2 else last_base, rows_dev), :]

    locals_ = [
        pltpu.make_async_copy(own_sources[s], shard_of(s), local_sem.at[s]) for s in range(5)
    ]

    @pl.when(c == 1)
    def _():
        for copy in locals_:
            copy.start()
        zero_lo = pl.multiple_of((1 - x) * half, 16)
        for l in range(2):
            w[l, pl.ds(zero_lo, pad), :] = jnp.zeros((pad, channels), w.dtype)

    dests = [lax.div(shuffle_ref[i], images) for i in range(images)]
    keys_local.wait()
    for e in range(n_dp):
        chosen = jnp.int32(0)
        for i in range(images):
            chosen = jnp.where(dests[i] == e, i, chosen)
        ksend[e] = keysv[chosen]

    pl.semaphore_wait(barrier, 2 * n_dp + 1 + c * (n_dp - 1))

    def remote(src, dst, send, recv, fsdp, dp=None):
        return pltpu.make_async_remote_copy(
            src_ref=src,
            dst_ref=dst,
            send_sem=send,
            recv_sem=recv,
            device_id={"dp": me if dp is None else dp, "fsdp": fsdp},
            device_id_type=MESH,
        )

    def key_copy(k, side):
        target = lax.rem(me + k, n_dp)
        column, lo = ((hub, own_lo), (peer_hub, peer_lo))[side]
        return remote(
            ksend.at[target, :, pl.ds(lo, window)],
            kbuf.at[c, x, me],
            key_send_sem.at[side, k],
            key_recv_sem.at[c],
            column,
            target,
        )

    pair = [
        remote(own_sources[s], shard_of(s), pair_send_sem.at[s], pair_recv_sem.at[s], hub)
        for s in range(5)
    ]

    def cross(s):
        source = own_sources[s].at[pl.ds(pl.multiple_of(lax.rem(me, 2) * piece, 16), piece), :]
        dst = {2: relay_red, 3: relay_exp, 4: relay_w}[s]
        return remote(source, dst, cross_send_sem.at[s - 2], cross_recv_sem.at[s - 2], peer_even)

    crosses = [cross(s) for s in (2, 3, 4)]
    sends_piece = c == quarter // 2

    def key_order():
        return [(k, side) for k in (*range(1, n_dp), 0) for side in (1, 0)]

    @pl.when(c == 0)
    def _():
        pair[0].start()
        for k, side in key_order():
            key_copy(k, side).start()
        for s in range(1, 5):
            pair[s].start()

    @pl.when(c == 1)
    def _():
        for k, side in key_order():
            if k > 0 or side > 0:
                key_copy(k, side).start()
        pltpu.make_async_copy(
            ksend.at[me, :, pl.ds(own_lo, window)], kbuf.at[1, x, me], key_recv_sem.at[1]
        ).start()

    @pl.when(sends_piece)
    def _():
        for copy in crosses:
            copy.start()

    relays = [relay_red, relay_exp, relay_w]

    def spread(t, j):
        whole = (red, exp, w_last)[t]
        lo = pl.multiple_of((1 - x) * half + quarter * piece, 16)
        return remote(
            relays[t],
            whole.at[pl.ds(lo, piece), :],
            spread_send_sem.at[t, j],
            spread_recv_sem.at[t, quarter],
            hub,
            square + lax.rem(quarter + j, 4),
        )

    def spread_arrived(t, q):
        whole = (red, exp, w_last)[t]
        lo = pl.multiple_of((1 - x) * half + q * piece, 16)
        remote(
            relays[t],
            whole.at[pl.ds(lo, piece), :],
            spread_send_sem.at[t, 0],
            spread_recv_sem.at[t, q],
            hub,
        ).wait_recv()

    @pl.when(c == 0)
    def _():
        for t in range(3):
            crosses[t].wait_recv()
            for j in range(4):
                spread(t, j).start()
        for k, side in key_order():
            key_copy(k, side).wait_send()
        for copy in pair:
            copy.wait_send()
        for t in range(3):
            for j in range(4):
                spread(t, j).wait_send()

    def back_copy(g, k):
        target = lax.rem(me + k, n_dp)
        if g == 1 and k == 0:
            return pltpu.make_async_copy(nsend.at[g, me], nrecv.at[me], back_recv_sem)
        return remote(
            nsend.at[g, target],
            nrecv.at[me],
            back_send_sem.at[g, k],
            back_recv_sem,
            2 * x + g,
            target,
        )

    def have(s):
        locals_[s].wait()
        pair[s].wait_recv()

    def have_full(t):
        have(t + 2)
        for q in range(4):
            spread_arrived(t, q)

    @pl.when(c == 1)
    def _():
        narrow = [
            remote(psend.at[g], precv.at[g], narrow_sem.at[0, g], narrow_sem.at[1, g], peer_hub)
            for g in range(2)
        ]
        wide = [
            remote(rsend.at[g], rrecv.at[g], wide_sem.at[0, g], wide_sem.at[1, g], peer_hub)
            for g in range(2)
        ]
        have(0)
        mines = [None, None]
        for g in ORDER:
            remote(
                kbuf.at[g], kbuf.at[g], key_send_sem.at[0, 0], key_recv_sem.at[g], hub
            ).wait_recv()
            entry = (
                kbuf[g].astype(jnp.float32).reshape(2 * rows, window).astype(jnp.bfloat16)
            )
            theirs = jnp.dot(
                entry, w[0, :, pl.ds(peer_lo, window)], preferred_element_type=jnp.float32
            )
            psend[g] = theirs.astype(jnp.bfloat16)
            narrow[g].start()
            mines[g] = jnp.dot(
                entry, w[0, :, pl.ds(own_lo, window)], preferred_element_type=jnp.float32
            )
        have(1)
        for g in ORDER:
            narrow[g].wait_recv()
            full = mines[g] + precv[g].astype(jnp.float32)
            entry = jnp.maximum(full, 0.0).astype(jnp.bfloat16)
            both = jnp.dot(entry, w[1], preferred_element_type=jnp.float32)
            low, high = both[:rows], both[rows:]
            rsend[g] = jnp.where(x == 0, high, low).astype(jnp.bfloat16)
            wide[g].start()
            mines[g] = jnp.where(x == 0, low, high)
        for k, side in key_order():
            if k > 0 or side > 0:
                key_copy(k, side).wait_send()
        have_full(0)
        have_full(1)
        scaled = [None, None]
        for g in ORDER:
            wide[g].wait_recv()
            full = mines[g] + rrecv[g].astype(jnp.float32)
            entry = jnp.maximum(full, 0.0).astype(jnp.bfloat16)
            spots = entry.astype(jnp.float32).reshape(images, positions, channels)
            pooled = (jnp.sum(spots, axis=1) * (1.0 / positions)).astype(jnp.bfloat16)
            squeeze_act = jnp.maximum(
                jnp.dot(pooled, red[...], preferred_element_type=jnp.float32), 0.0
            ).astype(jnp.bfloat16)
            excite = jax.nn.sigmoid(
                lax.dot_general(
                    squeeze_act,
                    exp[...],
                    (((1,), (1,)), ((), ())),
                    preferred_element_type=jnp.float32,
                )
            )
            scaled[g] = (
                (spots * excite[:, None, :]).reshape(rows, channels).astype(jnp.bfloat16)
            )
            if g == ORDER[0]:
                have_full(2)
            projected = jnp.dot(scaled[g], w_last[...], preferred_element_type=jnp.float32)
            mean_rows = jnp.sum(projected, axis=0, keepdims=True) / rows
            squares = jnp.sum(projected * projected, axis=0, keepdims=True) / rows
            scale_rows = lax.rsqrt(squares - mean_rows * mean_rows + epsilon) * gain_ref[
                ...
            ].reshape(1, channels)
            normed = (projected - mean_rows) * scale_rows + bias_ref[...].reshape(1, channels)
            nsend[g] = normed.reshape(images, positions, channels).astype(jnp.bfloat16)
            for k in (*range(1, n_dp), 0):
                back_copy(g, k).start()
        for g in range(2):
            narrow[g].wait_send()
            wide[g].wait_send()

    @pl.when(sends_piece)
    def _():
        for copy in crosses:
            copy.wait_send()

    remote(nrecv, nrecv, back_send_sem.at[0, 0], back_recv_sem, hub).wait_recv()
    for i in range(images):
        out_ref[i] = nrecv[dests[i]]

    @pl.when(c == 1)
    def _():
        for g in range(2):
            for k in range(n_dp):
                if g == 0 or k > 0:
                    back_copy(g, k).wait_send()


def local_fused(n_dp, keys, residual, se_reduce, se_expand, conv_weight, bn_gain, bn_bias, shuffle, unshuffle):
    images, positions, channels = keys.shape
    layers, rows_dev, _ = conv_weight.shape
    units = se_reduce.shape[1]
    rows = images * positions
    half = 2 * rows_dev
    piece = half // 4
    window = -(-half // lane) * lane
    bf16, f32 = jnp.bfloat16, jnp.float32
    vmem = pl.BlockSpec(memory_space=pltpu.VMEM)
    anywhere = pl.BlockSpec(memory_space=pl.ANY)
    dma = pltpu.SemaphoreType.DMA
    normed = pl.pallas_call(
        functools.partial(fused_kernel, n_dp, images, positions),
        out_shape=pltpu.VMEM((images, positions, channels), bf16),
        in_specs=[anywhere] * 4 + [vmem] * 2 + [pl.BlockSpec(memory_space=pltpu.SMEM)],
        out_specs=vmem,
        scratch_shapes=[
            pltpu.VMEM((2, window, channels), bf16),
            pltpu.VMEM((2 * half, channels), bf16),
            pltpu.VMEM((2 * half, units), bf16),
            pltpu.VMEM((2 * half, units), bf16),
            pltpu.VMEM((piece, channels), bf16),
            pltpu.VMEM((piece, units), bf16),
            pltpu.VMEM((piece, units), bf16),
            pltpu.VMEM((2, 2, images, positions, window), bf16),
            pltpu.VMEM((2, 2 * rows, window), bf16),
            pltpu.VMEM((2, 2 * rows, window), bf16),
            pltpu.VMEM((2, rows, channels), bf16),
            pltpu.VMEM((2, rows, channels), bf16),
            pltpu.VMEM((images, positions, channels), bf16),
            pltpu.VMEM((n_dp, positions, channels), bf16),
            pltpu.VMEM((2, images, positions, channels), bf16),
            pltpu.VMEM((n_dp, positions, channels), bf16),
            dma,
            dma((2, n_dp)),
            dma((2,)),
            dma((5,)),
            dma((5,)),
            dma((5,)),
            dma((3,)),
            dma((3,)),
            dma((3, 4)),
            dma((3, 4)),
            dma((2, 2)),
            dma((2, 2)),
            dma((2, n_dp)),
            dma,
        ],
        compiler_params=pltpu.CompilerParams(collective_id=0, has_side_effects=True),
        name="fused_encoder",
    )(
        keys,
        se_reduce,
        se_expand,
        conv_weight,
        bn_gain,
        bn_bias,
        shuffle,
    )
    encoded = jax.nn.relu(normed.astype(f32) + residual.astype(f32))
    return encoded.astype(bf16)


def solution(mesh):
    placed = (
        P(("dp", "fsdp"), None, None),
        P(("dp", "fsdp"), None, None),
        P("fsdp", None),
        P("fsdp", None),
        P(None, "fsdp", None),
        P(),
        P(),
        P(("dp", "fsdp")),
        P(("dp", "fsdp")),
    )
    n_dp, n_fsdp = mesh.shape["dp"], mesh.shape["fsdp"]

    def local(keys, *others):
        if n_fsdp == 4 and n_dp % 4 == 0 and keys.shape[0] == n_dp:
            return local_fused(n_dp, keys, *others)
        return local_general(keys, *others)

    return jax.shard_map(
        local, mesh=mesh, in_specs=placed, out_specs=P(("dp", "fsdp"), None, None), check_vma=False
    )
```

```python
import functools

import jax
import jax.numpy as jnp
from jax import lax
from jax.experimental import pallas as pl
from jax.experimental.pallas import tpu as pltpu
from jax.sharding import PartitionSpec as P

epsilon = 1e-05
lane = 128
MESH = pl.DeviceIdType.MESH


def project_rows(flat, weight_rows):
    return jnp.dot(
        flat,
        lax.all_gather(weight_rows, "fsdp", axis=0, tiled=True),
        preferred_element_type=jnp.float32,
    )


def reorder(images_block, order):
    images, positions, channels = images_block.shape
    chosen = (order[:, None] == jnp.arange(images)[None, :]).astype(images_block.dtype)
    picked = jnp.dot(
        chosen,
        images_block.reshape(images, positions * channels),
        preferred_element_type=jnp.float32,
    )
    return picked.astype(images_block.dtype).reshape(images_block.shape)


def encode_block(batch_block, reduce_full, expand_full, conv_weight):
    images, positions, channels = batch_block.shape
    layers = conv_weight.shape[0]
    flat = batch_block.reshape(images * positions, channels)
    for layer in range(layers - 1):
        flat = jax.nn.relu(project_rows(flat, conv_weight[layer])).astype(jnp.bfloat16)
    entry = flat.reshape(images, positions, channels)
    pooled = jnp.mean(entry, axis=1, dtype=jnp.float32).astype(jnp.bfloat16)
    squeeze_act = jax.nn.relu(
        jnp.dot(pooled, reduce_full, preferred_element_type=jnp.float32)
    ).astype(jnp.bfloat16)
    excite = jax.nn.sigmoid(
        lax.dot_general(
            squeeze_act, expand_full, (((1,), (1,)), ((), ())), preferred_element_type=jnp.float32
        )
    )
    scaled = (entry * excite[:, None, :]).astype(jnp.bfloat16).reshape(images * positions, channels)
    projected = project_rows(scaled, conv_weight[layers - 1])
    return projected.reshape(images, positions, channels)


def local_general(keys, residual, se_reduce, se_expand, conv_weight, bn_gain, bn_bias, shuffle, unshuffle):
    images, positions, channels = keys.shape
    count = images * positions
    reduce_full, expand_full = (
        lax.all_gather(se_reduce, "fsdp", axis=0, tiled=True),
        lax.all_gather(se_expand, "fsdp", axis=0, tiled=True),
    )
    send_order = jnp.argsort(shuffle)
    back_order = jnp.argsort(send_order)
    outgoing = reorder(keys, send_order)
    arrived = lax.all_to_all(outgoing, "dp", split_axis=0, concat_axis=0, tiled=True)
    projected = encode_block(arrived, reduce_full, expand_full, conv_weight)
    row_sums = jnp.sum(projected, axis=(0, 1))
    square_sums = jnp.sum(projected * projected, axis=(0, 1))
    mean_rows = row_sums / count
    variance = square_sums / count - mean_rows * mean_rows
    scale_rows = lax.rsqrt(variance + epsilon) * bn_gain
    normed_here = ((projected - mean_rows) * scale_rows + bn_bias).astype(jnp.bfloat16)
    returned = lax.all_to_all(normed_here, "dp", split_axis=0, concat_axis=0, tiled=True)
    normed = reorder(returned, back_order)
    encoded = jax.nn.relu(normed.astype(jnp.float32) + residual.astype(jnp.float32))
    return encoded.astype(jnp.bfloat16)


ORDER = (0, 1)


def fused_kernel(
    n_dp,
    images,
    positions,
    keys_ref,
    reduce_ref,
    expand_ref,
    weight_ref,
    gain_ref,
    bias_ref,
    shuffle_ref,
    out_ref,
    w,
    w_last,
    red,
    exp,
    relay_w,
    relay_red,
    relay_exp,
    kbuf,
    psend,
    precv,
    rsend,
    rrecv,
    keysv,
    ksend,
    nsend,
    nrecv,
    gain,
    bias,
    places,
    key_sem,
    key_send_sem,
    key_recv_sem,
    local_sem,
    pair_send_sem,
    pair_recv_sem,
    cross_send_sem,
    cross_recv_sem,
    spread_send_sem,
    spread_recv_sem,
    narrow_sem,
    wide_sem,
    back_send_sem,
    back_recv_sem,
):
    me = lax.axis_index("dp")
    f = lax.axis_index("fsdp")
    x, c = f // 2, f % 2
    hub = 2 * x + 1
    peer_hub = 2 * (1 - x) + 1
    peer_even = 2 * (1 - x)
    layers, rows_dev, channels = weight_ref.shape
    half = 2 * rows_dev
    window = kbuf.shape[4]
    pad = window - half
    rows = images * positions
    piece = half // 4
    quarter = lax.rem(me, 4)
    own_lo = pl.multiple_of(x * (channels - window), lane)
    peer_lo = pl.multiple_of((1 - x) * (channels - window), lane)
    base = pl.multiple_of(x * pad + c * rows_dev, 16)
    last_base = pl.multiple_of(f * rows_dev, 16)

    barrier = pltpu.get_barrier_semaphore()

    def partner(k):
        target = me
        for bit in (4, 2, 1):
            if k & bit:
                target = target + bit - 2 * bit * lax.rem(target // bit, 2)
        return target

    far_first = tuple(range(n_dp - 1, -1, -1))

    def greet(dp, fsdp):
        pl.semaphore_signal(
            barrier, inc=1, device_id={"dp": dp, "fsdp": fsdp}, device_id_type=MESH
        )

    @pl.when(c == 1)
    def _():
        for k in far_first:
            target = partner(k)
            greet(target, peer_hub)
            greet(target, 2 * (1 - x))
            if k > 0:
                greet(target, hub)
            greet(target, 2 * x)

    @pl.when(c == 0)
    def _():
        for k in far_first:
            greet(partner(k), hub)
        greet(me, peer_even)
        greet(me, peer_hub)

    keys_local = pltpu.make_async_copy(keys_ref, keysv, key_sem.at[0])
    keys_local.start()
    places_local = pltpu.make_async_copy(shuffle_ref, places, key_sem.at[1])
    places_local.start()
    norm_local = [
        pltpu.make_async_copy(gain_ref, gain, key_sem.at[2]),
        pltpu.make_async_copy(bias_ref, bias, key_sem.at[3]),
    ]

    own_sources = [weight_ref.at[0], weight_ref.at[1], reduce_ref, expand_ref, weight_ref.at[2]]
    full_targets = [w.at[0], w.at[1], red, exp, w_last]

    def shard_of(s):
        return full_targets[s].at[pl.ds(base if s < 2 else last_base, rows_dev), :]

    locals_ = [
        pltpu.make_async_copy(own_sources[s], shard_of(s), local_sem.at[s]) for s in range(5)
    ]

    @pl.when(c == 1)
    def _():
        for copy in locals_ + norm_local:
            copy.start()
        zero_lo = pl.multiple_of((1 - x) * half, 16)
        for l in range(2):
            w[l, pl.ds(zero_lo, pad), :] = jnp.zeros((pad, channels), w.dtype)

    places_local.wait()
    dests = [lax.div(places[i], images) for i in range(images)]
    keys_local.wait()
    for e in range(n_dp):
        chosen = jnp.int32(0)
        for i in range(images):
            chosen = jnp.where(dests[i] == e, i, chosen)
        ksend[e] = keysv[chosen]

    pl.semaphore_wait(barrier, 2 * n_dp + 1 + c * (n_dp - 1))

    def remote(src, dst, send, recv, fsdp, dp=None):
        return pltpu.make_async_remote_copy(
            src_ref=src,
            dst_ref=dst,
            send_sem=send,
            recv_sem=recv,
            device_id={"dp": me if dp is None else dp, "fsdp": fsdp},
            device_id_type=MESH,
        )

    def key_copy(k, side):
        target = partner(k)
        column, lo = ((hub, own_lo), (peer_hub, peer_lo))[side]
        return remote(
            ksend.at[target, :, pl.ds(lo, window)],
            kbuf.at[c, x, me],
            key_send_sem.at[side, k],
            key_recv_sem.at[c],
            column,
            target,
        )

    pair = [
        remote(own_sources[s], shard_of(s), pair_send_sem.at[s], pair_recv_sem.at[s], hub)
        for s in range(5)
    ]

    def cross(s):
        source = own_sources[s].at[pl.ds(pl.multiple_of(lax.rem(me, 2) * piece, 16), piece), :]
        dst = {2: relay_red, 3: relay_exp, 4: relay_w}[s]
        return remote(source, dst, cross_send_sem.at[s - 2], cross_recv_sem.at[s - 2], peer_even)

    crosses = [cross(s) for s in (2, 3, 4)]
    sends_piece = c == quarter // 2

    def key_order():
        return [(k, side) for k in far_first for side in (1, 0)]

    @pl.when(c == 0)
    def _():
        pair[0].start()
        for k, side in key_order():
            key_copy(k, side).start()

    @pl.when(c == 1)
    def _():
        for k, side in key_order():
            if k > 0 or side > 0:
                key_copy(k, side).start()
        pltpu.make_async_copy(
            ksend.at[me, :, pl.ds(own_lo, window)], kbuf.at[1, x, me], key_recv_sem.at[1]
        ).start()

    @pl.when(sends_piece)
    def _():
        for copy in crosses:
            copy.start()

    @pl.when(c == 0)
    def _():
        for copy in pair[1:]:
            copy.start()

    relays = [relay_red, relay_exp, relay_w]

    def spread(t, j):
        whole = (red, exp, w_last)[t]
        lo = pl.multiple_of((1 - x) * half + quarter * piece, 16)
        return remote(
            relays[t],
            whole.at[pl.ds(lo, piece), :],
            spread_send_sem.at[t, j],
            spread_recv_sem.at[t, quarter],
            hub,
            partner(j),
        )

    def spread_arrived(t, q):
        whole = (red, exp, w_last)[t]
        lo = pl.multiple_of((1 - x) * half + q * piece, 16)
        remote(
            relays[t],
            whole.at[pl.ds(lo, piece), :],
            spread_send_sem.at[t, 0],
            spread_recv_sem.at[t, q],
            hub,
        ).wait_recv()

    @pl.when(c == 0)
    def _():
        for t in range(3):
            crosses[t].wait_recv()
            for j in (3, 2, 1, 0):
                spread(t, j).start()
        for k, side in key_order():
            key_copy(k, side).wait_send()
        for copy in pair:
            copy.wait_send()
        for t in range(3):
            for j in range(4):
                spread(t, j).wait_send()

    def back_copy(g, k):
        target = partner(k)
        if g == 1 and k == 0:
            return pltpu.make_async_copy(nsend.at[g, me], nrecv.at[me], back_recv_sem)
        return remote(
            nsend.at[g, target],
            nrecv.at[me],
            back_send_sem.at[g, k],
            back_recv_sem,
            2 * x + g,
            target,
        )

    def have(s):
        locals_[s].wait()
        pair[s].wait_recv()

    def have_full(t):
        have(t + 2)
        for q in range(4):
            spread_arrived(t, q)

    @pl.when(c == 1)
    def _():
        narrow = [
            remote(psend.at[g], precv.at[g], narrow_sem.at[0, g], narrow_sem.at[1, g], peer_hub)
            for g in range(2)
        ]
        wide = [
            remote(rsend.at[g], rrecv.at[g], wide_sem.at[0, g], wide_sem.at[1, g], peer_hub)
            for g in range(2)
        ]
        have(0)
        mines = [None, None]
        entries = [None, None]
        for g in ORDER:
            remote(
                kbuf.at[g], kbuf.at[g], key_send_sem.at[0, 0], key_recv_sem.at[g], hub
            ).wait_recv()
            entries[g] = (
                kbuf[g].astype(jnp.float32).reshape(2 * rows, window).astype(jnp.bfloat16)
            )
            theirs = jnp.dot(
                entries[g], w[0, :, pl.ds(peer_lo, window)], preferred_element_type=jnp.float32
            )
            psend[g] = theirs.astype(jnp.bfloat16)
            narrow[g].start()
        for g in ORDER:
            mines[g] = jnp.dot(
                entries[g], w[0, :, pl.ds(own_lo, window)], preferred_element_type=jnp.float32
            )
        have(1)
        for g in ORDER:
            narrow[g].wait_recv()
            full = mines[g] + precv[g].astype(jnp.float32)
            entry = jnp.maximum(full, 0.0).astype(jnp.bfloat16)
            both = jnp.dot(entry, w[1], preferred_element_type=jnp.float32)
            low, high = both[:rows], both[rows:]
            rsend[g] = jnp.where(x == 0, high, low).astype(jnp.bfloat16)
            wide[g].start()
            mines[g] = jnp.where(x == 0, low, high)
        for k, side in key_order():
            if k > 0 or side > 0:
                key_copy(k, side).wait_send()
        have_full(0)
        have_full(1)
        for copy in norm_local:
            copy.wait()
        scaled = [None, None]
        for g in ORDER:
            wide[g].wait_recv()
            full = mines[g] + rrecv[g].astype(jnp.float32)
            entry = jnp.maximum(full, 0.0).astype(jnp.bfloat16)
            spots = entry.astype(jnp.float32).reshape(images, positions, channels)
            pooled = (jnp.sum(spots, axis=1) * (1.0 / positions)).astype(jnp.bfloat16)
            squeeze_act = jnp.maximum(
                jnp.dot(pooled, red[...], preferred_element_type=jnp.float32), 0.0
            ).astype(jnp.bfloat16)
            excite = jax.nn.sigmoid(
                lax.dot_general(
                    squeeze_act,
                    exp[...],
                    (((1,), (1,)), ((), ())),
                    preferred_element_type=jnp.float32,
                )
            )
            scaled[g] = (
                (spots * excite[:, None, :]).reshape(rows, channels).astype(jnp.bfloat16)
            )
            if g == ORDER[0]:
                have_full(2)
            projected = jnp.dot(scaled[g], w_last[...], preferred_element_type=jnp.float32)
            mean_rows = jnp.sum(projected, axis=0, keepdims=True) / rows
            squares = jnp.sum(projected * projected, axis=0, keepdims=True) / rows
            scale_rows = lax.rsqrt(squares - mean_rows * mean_rows + epsilon) * gain[
                ...
            ].reshape(1, channels)
            normed = (projected - mean_rows) * scale_rows + bias[...].reshape(1, channels)
            nsend[g] = normed.reshape(images, positions, channels).astype(jnp.bfloat16)
            for k in far_first:
                back_copy(g, k).start()
        for g in range(2):
            narrow[g].wait_send()
            wide[g].wait_send()

    @pl.when(sends_piece)
    def _():
        for copy in crosses:
            copy.wait_send()

    remote(nrecv, nrecv, back_send_sem.at[0, 0], back_recv_sem, hub).wait_recv()
    for i in range(images):
        out_ref[i] = nrecv[dests[i]]

    @pl.when(c == 1)
    def _():
        for g in range(2):
            for k in range(n_dp):
                if g == 0 or k > 0:
                    back_copy(g, k).wait_send()


def local_fused(n_dp, keys, residual, se_reduce, se_expand, conv_weight, bn_gain, bn_bias, shuffle, unshuffle):
    images, positions, channels = keys.shape
    layers, rows_dev, _ = conv_weight.shape
    units = se_reduce.shape[1]
    rows = images * positions
    half = 2 * rows_dev
    piece = half // 4
    window = -(-half // lane) * lane
    bf16, f32 = jnp.bfloat16, jnp.float32
    vmem = pl.BlockSpec(memory_space=pltpu.VMEM)
    anywhere = pl.BlockSpec(memory_space=pl.ANY)
    dma = pltpu.SemaphoreType.DMA
    normed = pl.pallas_call(
        functools.partial(fused_kernel, n_dp, images, positions),
        out_shape=pltpu.VMEM((images, positions, channels), bf16),
        in_specs=[anywhere] * 7,
        out_specs=vmem,
        scratch_shapes=[
            pltpu.VMEM((2, window, channels), bf16),
            pltpu.VMEM((2 * half, channels), bf16),
            pltpu.VMEM((2 * half, units), bf16),
            pltpu.VMEM((2 * half, units), bf16),
            pltpu.VMEM((piece, channels), bf16),
            pltpu.VMEM((piece, units), bf16),
            pltpu.VMEM((piece, units), bf16),
            pltpu.VMEM((2, 2, images, positions, window), bf16),
            pltpu.VMEM((2, 2 * rows, window), bf16),
            pltpu.VMEM((2, 2 * rows, window), bf16),
            pltpu.VMEM((2, rows, channels), bf16),
            pltpu.VMEM((2, rows, channels), bf16),
            pltpu.VMEM((images, positions, channels), bf16),
            pltpu.VMEM((n_dp, positions, channels), bf16),
            pltpu.VMEM((2, images, positions, channels), bf16),
            pltpu.VMEM((n_dp, positions, channels), bf16),
            pltpu.VMEM((channels,), f32),
            pltpu.VMEM((channels,), f32),
            pltpu.SMEM((images,), jnp.int32),
            dma((4,)),
            dma((2, n_dp)),
            dma((2,)),
            dma((5,)),
            dma((5,)),
            dma((5,)),
            dma((3,)),
            dma((3,)),
            dma((3, 4)),
            dma((3, 4)),
            dma((2, 2)),
            dma((2, 2)),
            dma((2, n_dp)),
            dma,
        ],
        compiler_params=pltpu.CompilerParams(collective_id=0, has_side_effects=True),
        name="fused_encoder",
    )(
        keys,
        se_reduce,
        se_expand,
        conv_weight,
        bn_gain,
        bn_bias,
        shuffle,
    )
    encoded = jax.nn.relu(normed.astype(f32) + residual.astype(f32))
    return encoded.astype(bf16)


def solution(mesh):
    placed = (
        P(("dp", "fsdp"), None, None),
        P(("dp", "fsdp"), None, None),
        P("fsdp", None),
        P("fsdp", None),
        P(None, "fsdp", None),
        P(),
        P(),
        P(("dp", "fsdp")),
        P(("dp", "fsdp")),
    )
    n_dp, n_fsdp = mesh.shape["dp"], mesh.shape["fsdp"]

    def local(keys, *others):
        if n_fsdp == 4 and n_dp == 8 and keys.shape[0] == n_dp:
            return local_fused(n_dp, keys, *others)
        return local_general(keys, *others)

    return jax.shard_map(
        local, mesh=mesh, in_specs=placed, out_specs=P(("dp", "fsdp"), None, None), check_vma=False
    )
```

```python
import functools

import jax
import jax.numpy as jnp
from jax import lax
from jax.experimental import pallas as pl
from jax.experimental.pallas import tpu as pltpu
from jax.sharding import PartitionSpec as P

epsilon = 1e-05
lane = 128
MESH = pl.DeviceIdType.MESH


def project_rows(flat, weight_rows):
    return jnp.dot(
        flat,
        lax.all_gather(weight_rows, "fsdp", axis=0, tiled=True),
        preferred_element_type=jnp.float32,
    )


def reorder(images_block, order):
    images, positions, channels = images_block.shape
    chosen = (order[:, None] == jnp.arange(images)[None, :]).astype(images_block.dtype)
    picked = jnp.dot(
        chosen,
        images_block.reshape(images, positions * channels),
        preferred_element_type=jnp.float32,
    )
    return picked.astype(images_block.dtype).reshape(images_block.shape)


def encode_block(batch_block, reduce_full, expand_full, conv_weight):
    images, positions, channels = batch_block.shape
    layers = conv_weight.shape[0]
    flat = batch_block.reshape(images * positions, channels)
    for layer in range(layers - 1):
        flat = jax.nn.relu(project_rows(flat, conv_weight[layer])).astype(jnp.bfloat16)
    entry = flat.reshape(images, positions, channels)
    pooled = jnp.mean(entry, axis=1, dtype=jnp.float32).astype(jnp.bfloat16)
    squeeze_act = jax.nn.relu(
        jnp.dot(pooled, reduce_full, preferred_element_type=jnp.float32)
    ).astype(jnp.bfloat16)
    excite = jax.nn.sigmoid(
        lax.dot_general(
            squeeze_act, expand_full, (((1,), (1,)), ((), ())), preferred_element_type=jnp.float32
        )
    )
    scaled = (entry * excite[:, None, :]).astype(jnp.bfloat16).reshape(images * positions, channels)
    projected = project_rows(scaled, conv_weight[layers - 1])
    return projected.reshape(images, positions, channels)


def local_general(keys, residual, se_reduce, se_expand, conv_weight, bn_gain, bn_bias, shuffle, unshuffle):
    images, positions, channels = keys.shape
    count = images * positions
    reduce_full, expand_full = (
        lax.all_gather(se_reduce, "fsdp", axis=0, tiled=True),
        lax.all_gather(se_expand, "fsdp", axis=0, tiled=True),
    )
    send_order = jnp.argsort(shuffle)
    back_order = jnp.argsort(send_order)
    outgoing = reorder(keys, send_order)
    arrived = lax.all_to_all(outgoing, "dp", split_axis=0, concat_axis=0, tiled=True)
    projected = encode_block(arrived, reduce_full, expand_full, conv_weight)
    row_sums = jnp.sum(projected, axis=(0, 1))
    square_sums = jnp.sum(projected * projected, axis=(0, 1))
    mean_rows = row_sums / count
    variance = square_sums / count - mean_rows * mean_rows
    scale_rows = lax.rsqrt(variance + epsilon) * bn_gain
    normed_here = ((projected - mean_rows) * scale_rows + bn_bias).astype(jnp.bfloat16)
    returned = lax.all_to_all(normed_here, "dp", split_axis=0, concat_axis=0, tiled=True)
    normed = reorder(returned, back_order)
    encoded = jax.nn.relu(normed.astype(jnp.float32) + residual.astype(jnp.float32))
    return encoded.astype(jnp.bfloat16)


ORDER = (0, 1)


def fused_kernel(
    n_dp,
    images,
    positions,
    keys_ref,
    reduce_ref,
    expand_ref,
    weight_ref,
    gain_ref,
    bias_ref,
    shuffle_ref,
    out_ref,
    w,
    w_last,
    red,
    exp,
    relay_w,
    relay_red,
    relay_exp,
    kbuf,
    psend,
    precv,
    rsend,
    rrecv,
    keysv,
    ksend,
    nsend,
    nrecv,
    gain,
    bias,
    places,
    key_sem,
    key_send_sem,
    key_recv_sem,
    local_sem,
    pair_send_sem,
    pair_recv_sem,
    cross_send_sem,
    cross_recv_sem,
    spread_send_sem,
    spread_recv_sem,
    narrow_sem,
    wide_sem,
    back_send_sem,
    back_recv_sem,
):
    me = lax.axis_index("dp")
    f = lax.axis_index("fsdp")
    x, c = f // 2, f % 2
    hub = 2 * x + 1
    peer_hub = 2 * (1 - x) + 1
    peer_even = 2 * (1 - x)
    layers, rows_dev, channels = weight_ref.shape
    half = 2 * rows_dev
    window = kbuf.shape[4]
    pad = window - half
    rows = images * positions
    piece = half // 4
    first = -(-piece // 32) * 16
    parts = ((0, piece), (0, piece), (0, first), (first, piece - first))
    quarter = lax.rem(me, 4)
    own_lo = pl.multiple_of(x * (channels - window), lane)
    peer_lo = pl.multiple_of((1 - x) * (channels - window), lane)
    base = pl.multiple_of(x * pad + c * rows_dev, 16)
    last_base = pl.multiple_of(f * rows_dev, 16)

    barrier = pltpu.get_barrier_semaphore()

    def partner(k):
        target = me
        for bit in (4, 2, 1):
            if k & bit:
                target = target + bit - 2 * bit * lax.rem(target // bit, 2)
        return target

    far_first = tuple(range(n_dp - 1, -1, -1))

    def greet(dp, fsdp):
        pl.semaphore_signal(
            barrier, inc=1, device_id={"dp": dp, "fsdp": fsdp}, device_id_type=MESH
        )

    @pl.when(c == 1)
    def _():
        for k in far_first:
            target = partner(k)
            greet(target, peer_hub)
            greet(target, 2 * (1 - x))
            if k > 0:
                greet(target, hub)
            greet(target, 2 * x)

    @pl.when(c == 0)
    def _():
        for k in far_first:
            greet(partner(k), hub)
        greet(me, peer_even)
        greet(me, peer_hub)

    keys_local = pltpu.make_async_copy(keys_ref, keysv, key_sem.at[0])
    keys_local.start()
    places_local = pltpu.make_async_copy(shuffle_ref, places, key_sem.at[1])
    places_local.start()
    norm_local = [
        pltpu.make_async_copy(gain_ref, gain, key_sem.at[2]),
        pltpu.make_async_copy(bias_ref, bias, key_sem.at[3]),
    ]

    own_sources = [weight_ref.at[0], weight_ref.at[1], reduce_ref, expand_ref, weight_ref.at[2]]
    full_targets = [w.at[0], w.at[1], red, exp, w_last]

    def shard_of(s):
        return full_targets[s].at[pl.ds(base if s < 2 else last_base, rows_dev), :]

    locals_ = [
        pltpu.make_async_copy(own_sources[s], shard_of(s), local_sem.at[s]) for s in range(5)
    ]

    @pl.when(c == 1)
    def _():
        for copy in locals_ + norm_local:
            copy.start()
        zero_lo = pl.multiple_of((1 - x) * half, 16)
        for l in range(2):
            w[l, pl.ds(zero_lo, pad), :] = jnp.zeros((pad, channels), w.dtype)

    places_local.wait()
    dests = [lax.div(places[i], images) for i in range(images)]
    keys_local.wait()
    for e in range(n_dp):
        chosen = jnp.int32(0)
        for i in range(images):
            chosen = jnp.where(dests[i] == e, i, chosen)
        ksend[e] = keysv[chosen]

    pl.semaphore_wait(barrier, 2 * n_dp + 1 + c * (n_dp - 1))

    def remote(src, dst, send, recv, fsdp, dp=None):
        return pltpu.make_async_remote_copy(
            src_ref=src,
            dst_ref=dst,
            send_sem=send,
            recv_sem=recv,
            device_id={"dp": me if dp is None else dp, "fsdp": fsdp},
            device_id_type=MESH,
        )

    def key_copy(k, side):
        target = partner(k)
        column, lo = ((hub, own_lo), (peer_hub, peer_lo))[side]
        return remote(
            ksend.at[target, :, pl.ds(lo, window)],
            kbuf.at[c, x, me],
            key_send_sem.at[side, k],
            key_recv_sem.at[c, k // 4],
            column,
            target,
        )

    pair = [
        remote(own_sources[s], shard_of(s), pair_send_sem.at[s], pair_recv_sem.at[s], hub)
        for s in range(5)
    ]

    part_sources = (reduce_ref, expand_ref, weight_ref.at[2], weight_ref.at[2])
    part_relays = (relay_red, relay_exp, relay_w, relay_w)
    part_targets = (red, exp, w_last, w_last)

    def cross(t):
        at, size = parts[t]
        lo = pl.multiple_of(lax.rem(me, 2) * piece + at, 16)
        return remote(
            part_sources[t].at[pl.ds(lo, size), :],
            part_relays[t].at[pl.ds(at, size), :],
            cross_send_sem.at[t],
            cross_recv_sem.at[t],
            peer_even,
        )

    crosses = [cross(t) for t in range(4)]
    sends_piece = c == quarter // 2

    def key_order():
        return [(k, side) for k in far_first for side in (1, 0)]

    @pl.when(c == 0)
    def _():
        pair[0].start()
        for k, side in key_order():
            key_copy(k, side).start()

    @pl.when(c == 1)
    def _():
        for k, side in key_order():
            if k > 0 or side > 0:
                key_copy(k, side).start()
        pltpu.make_async_copy(
            ksend.at[me, :, pl.ds(own_lo, window)], kbuf.at[1, x, me], key_recv_sem.at[1, 0]
        ).start()

    @pl.when(sends_piece)
    def _():
        for copy in crosses:
            copy.start()

    @pl.when(c == 0)
    def _():
        for copy in pair[1:]:
            copy.start()

    def part_copy(t, q, j):
        at, size = parts[t]
        lo = pl.multiple_of((1 - x) * half + q * piece + at, 16)
        return remote(
            part_relays[t].at[pl.ds(at, size), :],
            part_targets[t].at[pl.ds(lo, size), :],
            spread_send_sem.at[t, j],
            spread_recv_sem.at[t, q],
            hub,
            partner(j),
        )

    @pl.when(c == 0)
    def _():
        for t in range(4):
            crosses[t].wait_recv()
            for j in (3, 2, 1, 0):
                part_copy(t, quarter, j).start()
        for k, side in key_order():
            key_copy(k, side).wait_send()
        for copy in pair:
            copy.wait_send()
        for t in range(4):
            for j in range(4):
                part_copy(t, quarter, j).wait_send()

    def half_start(far):
        near = me // 4
        return 4 * (1 - near if far else near)

    def back_copy(g, k):
        target = partner(k)
        slot = lax.rem(target, 4) + k // 4 * 4
        if g == 1 and k == 0:
            return pltpu.make_async_copy(nsend.at[g, slot], nrecv.at[me], back_recv_sem)
        return remote(
            nsend.at[g, slot],
            nrecv.at[me],
            back_send_sem.at[g, k],
            back_recv_sem,
            2 * x + g,
            target,
        )

    def have(s):
        locals_[s].wait()
        pair[s].wait_recv()

    def have_full(t):
        have(t + 2)
        for p in ((t,) if t < 2 else (2, 3)):
            for q in range(4):
                part_copy(p, q, 0).wait_recv()

    @pl.when(c == 1)
    def _():
        narrow = [
            remote(psend.at[j], precv.at[j], narrow_sem.at[0, j], narrow_sem.at[1, j], peer_hub)
            for j in range(4)
        ]
        wide = [
            remote(rsend.at[j], rrecv.at[j], wide_sem.at[0, j], wide_sem.at[1, j], peer_hub)
            for j in range(4)
        ]
        chunks = [(far, g, 2 * far + i) for far in range(2) for i, g in enumerate(ORDER)]
        half_rows = rows // 2
        have(0)
        mines = [None] * 4
        entries = [None] * 4
        for far in range(2):
            for _, g, j in chunks[2 * far : 2 * far + 2]:
                sources = pl.ds(pl.multiple_of(half_start(far), 4), 4)
                remote(
                    kbuf.at[g, :, sources],
                    kbuf.at[g, :, sources],
                    key_send_sem.at[0, 0],
                    key_recv_sem.at[g, far],
                    hub,
                ).wait_recv()
                entries[j] = (
                    kbuf[g, :, sources]
                    .astype(jnp.float32)
                    .reshape(rows, window)
                    .astype(jnp.bfloat16)
                )
                theirs = jnp.dot(
                    entries[j], w[0, :, pl.ds(peer_lo, window)], preferred_element_type=jnp.float32
                )
                psend[j] = theirs.astype(jnp.bfloat16)
                narrow[j].start()
            own = jnp.dot(
                jnp.concatenate(entries[2 * far : 2 * far + 2], axis=0),
                w[0, :, pl.ds(own_lo, window)],
                preferred_element_type=jnp.float32,
            )
            mines[2 * far], mines[2 * far + 1] = own[:rows], own[rows:]
        have(1)
        for _, g, j in chunks:
            narrow[j].wait_recv()
            full = mines[j] + precv[j].astype(jnp.float32)
            entry = jnp.maximum(full, 0.0).astype(jnp.bfloat16)
            both = jnp.dot(entry, w[1], preferred_element_type=jnp.float32)
            low, high = both[:half_rows], both[half_rows:]
            rsend[j] = jnp.where(x == 0, high, low).astype(jnp.bfloat16)
            wide[j].start()
            mines[j] = jnp.where(x == 0, low, high)
        for k, side in key_order():
            if k > 0 or side > 0:
                key_copy(k, side).wait_send()
        have_full(0)
        have_full(1)
        for copy in norm_local:
            copy.wait()
        scaled = [None, None]
        for i, g in enumerate(ORDER):
            settled = []
            for j in (i, i + 2):
                wide[j].wait_recv()
                full = mines[j] + rrecv[j].astype(jnp.float32)
                settled.append(jnp.maximum(full, 0.0).astype(jnp.bfloat16))
            entry = jnp.concatenate(settled, axis=0)
            spots = entry.astype(jnp.float32).reshape(images, positions, channels)
            pooled = (jnp.sum(spots, axis=1) * (1.0 / positions)).astype(jnp.bfloat16)
            squeeze_act = jnp.maximum(
                jnp.dot(pooled, red[...], preferred_element_type=jnp.float32), 0.0
            ).astype(jnp.bfloat16)
            excite = jax.nn.sigmoid(
                lax.dot_general(
                    squeeze_act,
                    exp[...],
                    (((1,), (1,)), ((), ())),
                    preferred_element_type=jnp.float32,
                )
            )
            scaled[g] = (
                (spots * excite[:, None, :]).reshape(rows, channels).astype(jnp.bfloat16)
            )
            if g == ORDER[0]:
                have_full(2)
            projected = jnp.dot(scaled[g], w_last[...], preferred_element_type=jnp.float32)
            mean_rows = jnp.sum(projected, axis=0, keepdims=True) / rows
            squares = jnp.sum(projected * projected, axis=0, keepdims=True) / rows
            scale_rows = lax.rsqrt(squares - mean_rows * mean_rows + epsilon) * gain[
                ...
            ].reshape(1, channels)
            normed = (projected - mean_rows) * scale_rows + bias[...].reshape(1, channels)
            nsend[g] = normed.reshape(images, positions, channels).astype(jnp.bfloat16)
            for k in far_first:
                back_copy(g, k).start()
        for j in range(4):
            narrow[j].wait_send()
            wide[j].wait_send()

    @pl.when(sends_piece)
    def _():
        for copy in crosses:
            copy.wait_send()

    remote(nrecv, nrecv, back_send_sem.at[0, 0], back_recv_sem, hub).wait_recv()
    for i in range(images):
        out_ref[i] = nrecv[dests[i]]

    @pl.when(c == 1)
    def _():
        for g in range(2):
            for k in range(n_dp):
                if g == 0 or k > 0:
                    back_copy(g, k).wait_send()


def local_fused(n_dp, keys, residual, se_reduce, se_expand, conv_weight, bn_gain, bn_bias, shuffle, unshuffle):
    images, positions, channels = keys.shape
    layers, rows_dev, _ = conv_weight.shape
    units = se_reduce.shape[1]
    rows = images * positions
    half = 2 * rows_dev
    piece = half // 4
    window = -(-half // lane) * lane
    bf16, f32 = jnp.bfloat16, jnp.float32
    vmem = pl.BlockSpec(memory_space=pltpu.VMEM)
    anywhere = pl.BlockSpec(memory_space=pl.ANY)
    dma = pltpu.SemaphoreType.DMA
    normed = pl.pallas_call(
        functools.partial(fused_kernel, n_dp, images, positions),
        out_shape=pltpu.VMEM((images, positions, channels), bf16),
        in_specs=[anywhere] * 7,
        out_specs=vmem,
        scratch_shapes=[
            pltpu.VMEM((2, window, channels), bf16),
            pltpu.VMEM((2 * half, channels), bf16),
            pltpu.VMEM((2 * half, units), bf16),
            pltpu.VMEM((2 * half, units), bf16),
            pltpu.VMEM((piece, channels), bf16),
            pltpu.VMEM((piece, units), bf16),
            pltpu.VMEM((piece, units), bf16),
            pltpu.VMEM((2, 2, images, positions, window), bf16),
            pltpu.VMEM((4, rows, window), bf16),
            pltpu.VMEM((4, rows, window), bf16),
            pltpu.VMEM((4, rows // 2, channels), bf16),
            pltpu.VMEM((4, rows // 2, channels), bf16),
            pltpu.VMEM((images, positions, channels), bf16),
            pltpu.VMEM((n_dp, positions, channels), bf16),
            pltpu.VMEM((2, images, positions, channels), bf16),
            pltpu.VMEM((n_dp, positions, channels), bf16),
            pltpu.VMEM((channels,), f32),
            pltpu.VMEM((channels,), f32),
            pltpu.SMEM((images,), jnp.int32),
            dma((4,)),
            dma((2, n_dp)),
            dma((2, 2)),
            dma((5,)),
            dma((5,)),
            dma((5,)),
            dma((4,)),
            dma((4,)),
            dma((4, 4)),
            dma((4, 4)),
            dma((2, 4)),
            dma((2, 4)),
            dma((2, n_dp)),
            dma,
        ],
        compiler_params=pltpu.CompilerParams(collective_id=0, has_side_effects=True),
        name="fused_encoder",
    )(
        keys,
        se_reduce,
        se_expand,
        conv_weight,
        bn_gain,
        bn_bias,
        shuffle,
    )
    encoded = jax.nn.relu(normed.astype(f32) + residual.astype(f32))
    return encoded.astype(bf16)


def solution(mesh):
    placed = (
        P(("dp", "fsdp"), None, None),
        P(("dp", "fsdp"), None, None),
        P("fsdp", None),
        P("fsdp", None),
        P(None, "fsdp", None),
        P(),
        P(),
        P(("dp", "fsdp")),
        P(("dp", "fsdp")),
    )
    n_dp, n_fsdp = mesh.shape["dp"], mesh.shape["fsdp"]

    def local(keys, *others):
        if n_fsdp == 4 and n_dp == 8 and keys.shape[0] == n_dp:
            return local_fused(n_dp, keys, *others)
        return local_general(keys, *others)

    return jax.shard_map(
        local, mesh=mesh, in_specs=placed, out_specs=P(("dp", "fsdp"), None, None), check_vma=False
    )
```

```python
import functools

import jax
import jax.numpy as jnp
from jax import lax
from jax.experimental import pallas as pl
from jax.experimental.pallas import tpu as pltpu
from jax.sharding import PartitionSpec as P

epsilon = 1e-05
lane = 128
MESH = pl.DeviceIdType.MESH


def project_rows(flat, weight_rows):
    return jnp.dot(
        flat,
        lax.all_gather(weight_rows, "fsdp", axis=0, tiled=True),
        preferred_element_type=jnp.float32,
    )


def reorder(images_block, order):
    images, positions, channels = images_block.shape
    chosen = (order[:, None] == jnp.arange(images)[None, :]).astype(images_block.dtype)
    picked = jnp.dot(
        chosen,
        images_block.reshape(images, positions * channels),
        preferred_element_type=jnp.float32,
    )
    return picked.astype(images_block.dtype).reshape(images_block.shape)


def encode_block(batch_block, reduce_full, expand_full, conv_weight):
    images, positions, channels = batch_block.shape
    layers = conv_weight.shape[0]
    flat = batch_block.reshape(images * positions, channels)
    for layer in range(layers - 1):
        flat = jax.nn.relu(project_rows(flat, conv_weight[layer])).astype(jnp.bfloat16)
    entry = flat.reshape(images, positions, channels)
    pooled = jnp.mean(entry, axis=1, dtype=jnp.float32).astype(jnp.bfloat16)
    squeeze_act = jax.nn.relu(
        jnp.dot(pooled, reduce_full, preferred_element_type=jnp.float32)
    ).astype(jnp.bfloat16)
    excite = jax.nn.sigmoid(
        lax.dot_general(
            squeeze_act, expand_full, (((1,), (1,)), ((), ())), preferred_element_type=jnp.float32
        )
    )
    scaled = (entry * excite[:, None, :]).astype(jnp.bfloat16).reshape(images * positions, channels)
    projected = project_rows(scaled, conv_weight[layers - 1])
    return projected.reshape(images, positions, channels)


def local_general(keys, residual, se_reduce, se_expand, conv_weight, bn_gain, bn_bias, shuffle, unshuffle):
    images, positions, channels = keys.shape
    count = images * positions
    reduce_full, expand_full = (
        lax.all_gather(se_reduce, "fsdp", axis=0, tiled=True),
        lax.all_gather(se_expand, "fsdp", axis=0, tiled=True),
    )
    send_order = jnp.argsort(shuffle)
    back_order = jnp.argsort(send_order)
    outgoing = reorder(keys, send_order)
    arrived = lax.all_to_all(outgoing, "dp", split_axis=0, concat_axis=0, tiled=True)
    projected = encode_block(arrived, reduce_full, expand_full, conv_weight)
    row_sums = jnp.sum(projected, axis=(0, 1))
    square_sums = jnp.sum(projected * projected, axis=(0, 1))
    mean_rows = row_sums / count
    variance = square_sums / count - mean_rows * mean_rows
    scale_rows = lax.rsqrt(variance + epsilon) * bn_gain
    normed_here = ((projected - mean_rows) * scale_rows + bn_bias).astype(jnp.bfloat16)
    returned = lax.all_to_all(normed_here, "dp", split_axis=0, concat_axis=0, tiled=True)
    normed = reorder(returned, back_order)
    encoded = jax.nn.relu(normed.astype(jnp.float32) + residual.astype(jnp.float32))
    return encoded.astype(jnp.bfloat16)


ORDER = (0, 1)


def fused_kernel(
    n_dp,
    images,
    positions,
    keys_ref,
    reduce_ref,
    expand_ref,
    weight_ref,
    gain_ref,
    bias_ref,
    shuffle_ref,
    out_ref,
    w,
    w_last,
    red,
    exp,
    relay_w,
    relay_red,
    relay_exp,
    kbuf,
    psend,
    precv,
    rsend,
    rrecv,
    keysv,
    ksend,
    nsend,
    nrecv,
    gain,
    bias,
    places,
    key_sem,
    key_send_sem,
    key_recv_sem,
    local_sem,
    pair_send_sem,
    pair_recv_sem,
    cross_send_sem,
    cross_recv_sem,
    spread_send_sem,
    spread_recv_sem,
    narrow_sem,
    wide_sem,
    back_send_sem,
    back_recv_sem,
):
    me = lax.axis_index("dp")
    f = lax.axis_index("fsdp")
    x, c = f // 2, f % 2
    hub = 2 * x + 1
    peer_hub = 2 * (1 - x) + 1
    peer_even = 2 * (1 - x)
    layers, rows_dev, channels = weight_ref.shape
    half = 2 * rows_dev
    window = kbuf.shape[4]
    pad = window - half
    rows = images * positions
    piece = half // 4
    parts = ((0, 32), (32, 80), (0, 112), (0, 32), (32, 48), (80, 32))
    quarter = lax.rem(me, 4)
    own_lo = pl.multiple_of(x * (channels - window), lane)
    peer_lo = pl.multiple_of((1 - x) * (channels - window), lane)
    base = pl.multiple_of(x * pad + c * rows_dev, 16)
    last_base = pl.multiple_of(f * rows_dev, 16)

    barrier = pltpu.get_barrier_semaphore()

    def partner(k):
        target = me
        for bit in (4, 2, 1):
            if k & bit:
                target = target + bit - 2 * bit * lax.rem(target // bit, 2)
        return target

    far_first = tuple(range(n_dp - 1, -1, -1))

    def greet(dp, fsdp):
        pl.semaphore_signal(
            barrier, inc=1, device_id={"dp": dp, "fsdp": fsdp}, device_id_type=MESH
        )

    @pl.when(c == 1)
    def _():
        for k in far_first:
            target = partner(k)
            greet(target, peer_hub)
            greet(target, 2 * (1 - x))
            if k > 0:
                greet(target, hub)
            greet(target, 2 * x)

    @pl.when(c == 0)
    def _():
        for k in far_first:
            greet(partner(k), hub)
        greet(me, peer_even)
        greet(me, peer_hub)

    keys_local = pltpu.make_async_copy(keys_ref, keysv, key_sem.at[0])
    keys_local.start()
    places_local = pltpu.make_async_copy(shuffle_ref, places, key_sem.at[1])
    places_local.start()
    norm_local = [
        pltpu.make_async_copy(gain_ref, gain, key_sem.at[2]),
        pltpu.make_async_copy(bias_ref, bias, key_sem.at[3]),
    ]

    own_sources = [weight_ref.at[0], weight_ref.at[1], reduce_ref, expand_ref, weight_ref.at[2]]
    full_targets = [w.at[0], w.at[1], red, exp, w_last]

    def shard_of(s):
        return full_targets[s].at[pl.ds(base if s < 2 else last_base, rows_dev), :]

    locals_ = [
        pltpu.make_async_copy(own_sources[s], shard_of(s), local_sem.at[s]) for s in range(5)
    ]

    @pl.when(c == 1)
    def _():
        for copy in locals_ + norm_local:
            copy.start()
        zero_lo = pl.multiple_of((1 - x) * half, 16)
        for l in range(2):
            w[l, pl.ds(zero_lo, pad), :] = jnp.zeros((pad, channels), w.dtype)

    places_local.wait()
    dests = [lax.div(places[i], images) for i in range(images)]
    keys_local.wait()
    for e in range(n_dp):
        chosen = jnp.int32(0)
        for i in range(images):
            chosen = jnp.where(dests[i] == e, i, chosen)
        ksend[e] = keysv[chosen]

    pl.semaphore_wait(barrier, 2 * n_dp + 1 + c * (n_dp - 1))

    def remote(src, dst, send, recv, fsdp, dp=None):
        return pltpu.make_async_remote_copy(
            src_ref=src,
            dst_ref=dst,
            send_sem=send,
            recv_sem=recv,
            device_id={"dp": me if dp is None else dp, "fsdp": fsdp},
            device_id_type=MESH,
        )

    def key_copy(k, side):
        target = partner(k)
        column, lo = ((hub, own_lo), (peer_hub, peer_lo))[side]
        return remote(
            ksend.at[target, :, pl.ds(lo, window)],
            kbuf.at[c, x, me],
            key_send_sem.at[side, k],
            key_recv_sem.at[c, k // 4],
            column,
            target,
        )

    pair = [
        remote(own_sources[s], shard_of(s), pair_send_sem.at[s], pair_recv_sem.at[s], hub)
        for s in range(5)
    ]

    part_sources = [(reduce_ref, expand_ref, weight_ref.at[2])[i] for i in [0, 0, 1, 2, 2, 2]]
    part_relays = [(relay_red, relay_exp, relay_w)[i] for i in [0, 0, 1, 2, 2, 2]]
    part_targets = [(red, exp, w_last)[i] for i in [0, 0, 1, 2, 2, 2]]

    def cross(t):
        at, size = parts[t]
        lo = pl.multiple_of(lax.rem(me, 2) * piece + at, 16)
        return remote(
            part_sources[t].at[pl.ds(lo, size), :],
            part_relays[t].at[pl.ds(at, size), :],
            cross_send_sem.at[t],
            cross_recv_sem.at[t],
            peer_even,
        )

    crosses = [cross(t) for t in range(6)]
    sends_piece = c == quarter // 2

    def key_order():
        return [(k, side) for k in far_first for side in (1, 0)]

    @pl.when(c == 0)
    def _():
        pair[0].start()
        for k, side in key_order():
            key_copy(k, side).start()

    @pl.when(c == 1)
    def _():
        for k, side in key_order():
            if k > 0 or side > 0:
                key_copy(k, side).start()
        pltpu.make_async_copy(
            ksend.at[me, :, pl.ds(own_lo, window)], kbuf.at[1, x, me], key_recv_sem.at[1, 0]
        ).start()

    @pl.when(sends_piece)
    def _():
        for copy in crosses:
            copy.start()

    @pl.when(c == 0)
    def _():
        for copy in pair[1:]:
            copy.start()

    def part_copy(t, q, j):
        at, size = parts[t]
        lo = pl.multiple_of((1 - x) * half + q * piece + at, 16)
        return remote(
            part_relays[t].at[pl.ds(at, size), :],
            part_targets[t].at[pl.ds(lo, size), :],
            spread_send_sem.at[t, j],
            spread_recv_sem.at[t, q],
            hub,
            partner(j),
        )

    @pl.when(c == 0)
    def _():
        for t in range(6):
            crosses[t].wait_recv()
            for j in (3, 2, 1, 0):
                part_copy(t, quarter, j).start()
        for k, side in key_order():
            key_copy(k, side).wait_send()
        for copy in pair:
            copy.wait_send()
        for t in range(6):
            for j in range(4):
                part_copy(t, quarter, j).wait_send()

    def half_start(far):
        near = me // 4
        return 4 * (1 - near if far else near)

    def back_copy(g, k):
        target = partner(k)
        slot = lax.rem(target, 4) + k // 4 * 4
        if g == 1 and k == 0:
            return pltpu.make_async_copy(nsend.at[g, slot], nrecv.at[me], back_recv_sem)
        return remote(
            nsend.at[g, slot],
            nrecv.at[me],
            back_send_sem.at[g, k],
            back_recv_sem,
            2 * x + g,
            target,
        )

    def have(s):
        locals_[s].wait()
        pair[s].wait_recv()

    def have_full(t):
        have(t + 2)
        for p in [p for p, i in enumerate([0, 0, 1, 2, 2, 2]) if i == t]:
            for q in range(4):
                part_copy(p, q, 0).wait_recv()

    @pl.when(c == 1)
    def _():
        narrow = [
            remote(psend.at[j], precv.at[j], narrow_sem.at[0, j], narrow_sem.at[1, j], peer_hub)
            for j in range(4)
        ]
        wide = [
            remote(rsend.at[j], rrecv.at[j], wide_sem.at[0, j], wide_sem.at[1, j], peer_hub)
            for j in range(4)
        ]
        chunks = [(far, g, 2 * far + i) for far in range(2) for i, g in enumerate(ORDER)]
        half_rows = rows // 2
        have(0)
        mines = [None] * 4
        entries = [None] * 4
        for far in range(2):
            for _, g, j in chunks[2 * far : 2 * far + 2]:
                sources = pl.ds(pl.multiple_of(half_start(far), 4), 4)
                remote(
                    kbuf.at[g, :, sources],
                    kbuf.at[g, :, sources],
                    key_send_sem.at[0, 0],
                    key_recv_sem.at[g, far],
                    hub,
                ).wait_recv()
                entries[j] = (
                    kbuf[g, :, sources]
                    .astype(jnp.float32)
                    .reshape(rows, window)
                    .astype(jnp.bfloat16)
                )
                theirs = jnp.dot(
                    entries[j], w[0, :, pl.ds(peer_lo, window)], preferred_element_type=jnp.float32
                )
                psend[j] = theirs.astype(jnp.bfloat16)
                narrow[j].start()
            own = jnp.dot(
                jnp.concatenate(entries[2 * far : 2 * far + 2], axis=0),
                w[0, :, pl.ds(own_lo, window)],
                preferred_element_type=jnp.float32,
            )
            mines[2 * far], mines[2 * far + 1] = own[:rows], own[rows:]
        have(1)
        for _, g, j in chunks:
            narrow[j].wait_recv()
            full = mines[j] + precv[j].astype(jnp.float32)
            entry = jnp.maximum(full, 0.0).astype(jnp.bfloat16)
            both = jnp.dot(entry, w[1], preferred_element_type=jnp.float32)
            low, high = both[:half_rows], both[half_rows:]
            rsend[j] = jnp.where(x == 0, high, low).astype(jnp.bfloat16)
            wide[j].start()
            mines[j] = jnp.where(x == 0, low, high)
        for k, side in key_order():
            if k > 0 or side > 0:
                key_copy(k, side).wait_send()
        have_full(0)
        have_full(1)
        for copy in norm_local:
            copy.wait()
        scaled = [None, None]
        for i, g in enumerate(ORDER):
            settled = []
            for j in (i, i + 2):
                wide[j].wait_recv()
                full = mines[j] + rrecv[j].astype(jnp.float32)
                settled.append(jnp.maximum(full, 0.0).astype(jnp.bfloat16))
            entry = jnp.concatenate(settled, axis=0)
            spots = entry.astype(jnp.float32).reshape(images, positions, channels)
            pooled = (jnp.sum(spots, axis=1) * (1.0 / positions)).astype(jnp.bfloat16)
            squeeze_act = jnp.maximum(
                jnp.dot(pooled, red[...], preferred_element_type=jnp.float32), 0.0
            ).astype(jnp.bfloat16)
            excite = jax.nn.sigmoid(
                lax.dot_general(
                    squeeze_act,
                    exp[...],
                    (((1,), (1,)), ((), ())),
                    preferred_element_type=jnp.float32,
                )
            )
            scaled[g] = (
                (spots * excite[:, None, :]).reshape(rows, channels).astype(jnp.bfloat16)
            )
            if g == ORDER[0]:
                have_full(2)
            projected = jnp.dot(scaled[g], w_last[...], preferred_element_type=jnp.float32)
            mean_rows = jnp.sum(projected, axis=0, keepdims=True) / rows
            squares = jnp.sum(projected * projected, axis=0, keepdims=True) / rows
            scale_rows = lax.rsqrt(squares - mean_rows * mean_rows + epsilon) * gain[
                ...
            ].reshape(1, channels)
            normed = (projected - mean_rows) * scale_rows + bias[...].reshape(1, channels)
            nsend[g] = normed.reshape(images, positions, channels).astype(jnp.bfloat16)
            for k in far_first:
                back_copy(g, k).start()
        for j in range(4):
            narrow[j].wait_send()
            wide[j].wait_send()

    @pl.when(sends_piece)
    def _():
        for copy in crosses:
            copy.wait_send()

    remote(nrecv, nrecv, back_send_sem.at[0, 0], back_recv_sem, hub).wait_recv()
    for i in range(images):
        out_ref[i] = nrecv[dests[i]]

    @pl.when(c == 1)
    def _():
        for g in range(2):
            for k in range(n_dp):
                if g == 0 or k > 0:
                    back_copy(g, k).wait_send()


def local_fused(n_dp, keys, residual, se_reduce, se_expand, conv_weight, bn_gain, bn_bias, shuffle, unshuffle):
    images, positions, channels = keys.shape
    layers, rows_dev, _ = conv_weight.shape
    units = se_reduce.shape[1]
    rows = images * positions
    half = 2 * rows_dev
    piece = half // 4
    window = -(-half // lane) * lane
    bf16, f32 = jnp.bfloat16, jnp.float32
    vmem = pl.BlockSpec(memory_space=pltpu.VMEM)
    anywhere = pl.BlockSpec(memory_space=pl.ANY)
    dma = pltpu.SemaphoreType.DMA
    normed = pl.pallas_call(
        functools.partial(fused_kernel, n_dp, images, positions),
        out_shape=pltpu.VMEM((images, positions, channels), bf16),
        in_specs=[anywhere] * 7,
        out_specs=vmem,
        scratch_shapes=[
            pltpu.VMEM((2, window, channels), bf16),
            pltpu.VMEM((2 * half, channels), bf16),
            pltpu.VMEM((2 * half, units), bf16),
            pltpu.VMEM((2 * half, units), bf16),
            pltpu.VMEM((piece, channels), bf16),
            pltpu.VMEM((piece, units), bf16),
            pltpu.VMEM((piece, units), bf16),
            pltpu.VMEM((2, 2, images, positions, window), bf16),
            pltpu.VMEM((4, rows, window), bf16),
            pltpu.VMEM((4, rows, window), bf16),
            pltpu.VMEM((4, rows // 2, channels), bf16),
            pltpu.VMEM((4, rows // 2, channels), bf16),
            pltpu.VMEM((images, positions, channels), bf16),
            pltpu.VMEM((n_dp, positions, channels), bf16),
            pltpu.VMEM((2, images, positions, channels), bf16),
            pltpu.VMEM((n_dp, positions, channels), bf16),
            pltpu.VMEM((channels,), f32),
            pltpu.VMEM((channels,), f32),
            pltpu.SMEM((images,), jnp.int32),
            dma((4,)),
            dma((2, n_dp)),
            dma((2, 2)),
            dma((5,)),
            dma((5,)),
            dma((5,)),
            dma((6,)),
            dma((6,)),
            dma((6, 4)),
            dma((6, 4)),
            dma((2, 4)),
            dma((2, 4)),
            dma((2, n_dp)),
            dma,
        ],
        compiler_params=pltpu.CompilerParams(collective_id=0, has_side_effects=True),
        name="fused_encoder",
    )(
        keys,
        se_reduce,
        se_expand,
        conv_weight,
        bn_gain,
        bn_bias,
        shuffle,
    )
    encoded = jax.nn.relu(normed.astype(f32) + residual.astype(f32))
    return encoded.astype(bf16)


def solution(mesh):
    placed = (
        P(("dp", "fsdp"), None, None),
        P(("dp", "fsdp"), None, None),
        P("fsdp", None),
        P("fsdp", None),
        P(None, "fsdp", None),
        P(),
        P(),
        P(("dp", "fsdp")),
        P(("dp", "fsdp")),
    )
    n_dp, n_fsdp = mesh.shape["dp"], mesh.shape["fsdp"]

    def local(keys, *others):
        if n_fsdp == 4 and n_dp == 8 and keys.shape[0] == n_dp:
            return local_fused(n_dp, keys, *others)
        return local_general(keys, *others)

    return jax.shard_map(
        local, mesh=mesh, in_specs=placed, out_specs=P(("dp", "fsdp"), None, None), check_vma=False
    )
```

```python
import functools

import jax
import jax.numpy as jnp
from jax import lax
from jax.experimental import pallas as pl
from jax.experimental.pallas import tpu as pltpu
from jax.sharding import PartitionSpec as P

epsilon = 1e-05
lane = 128
MESH = pl.DeviceIdType.MESH


def project_rows(flat, weight_rows):
    return jnp.dot(
        flat,
        lax.all_gather(weight_rows, "fsdp", axis=0, tiled=True),
        preferred_element_type=jnp.float32,
    )


def reorder(images_block, order):
    images, positions, channels = images_block.shape
    chosen = (order[:, None] == jnp.arange(images)[None, :]).astype(images_block.dtype)
    picked = jnp.dot(
        chosen,
        images_block.reshape(images, positions * channels),
        preferred_element_type=jnp.float32,
    )
    return picked.astype(images_block.dtype).reshape(images_block.shape)


def encode_block(batch_block, reduce_full, expand_full, conv_weight):
    images, positions, channels = batch_block.shape
    layers = conv_weight.shape[0]
    flat = batch_block.reshape(images * positions, channels)
    for layer in range(layers - 1):
        flat = jax.nn.relu(project_rows(flat, conv_weight[layer])).astype(jnp.bfloat16)
    entry = flat.reshape(images, positions, channels)
    pooled = jnp.mean(entry, axis=1, dtype=jnp.float32).astype(jnp.bfloat16)
    squeeze_act = jax.nn.relu(
        jnp.dot(pooled, reduce_full, preferred_element_type=jnp.float32)
    ).astype(jnp.bfloat16)
    excite = jax.nn.sigmoid(
        lax.dot_general(
            squeeze_act, expand_full, (((1,), (1,)), ((), ())), preferred_element_type=jnp.float32
        )
    )
    scaled = (entry * excite[:, None, :]).astype(jnp.bfloat16).reshape(images * positions, channels)
    projected = project_rows(scaled, conv_weight[layers - 1])
    return projected.reshape(images, positions, channels)


def local_general(keys, residual, se_reduce, se_expand, conv_weight, bn_gain, bn_bias, shuffle, unshuffle):
    images, positions, channels = keys.shape
    count = images * positions
    reduce_full, expand_full = (
        lax.all_gather(se_reduce, "fsdp", axis=0, tiled=True),
        lax.all_gather(se_expand, "fsdp", axis=0, tiled=True),
    )
    send_order = jnp.argsort(shuffle)
    back_order = jnp.argsort(send_order)
    outgoing = reorder(keys, send_order)
    arrived = lax.all_to_all(outgoing, "dp", split_axis=0, concat_axis=0, tiled=True)
    projected = encode_block(arrived, reduce_full, expand_full, conv_weight)
    row_sums = jnp.sum(projected, axis=(0, 1))
    square_sums = jnp.sum(projected * projected, axis=(0, 1))
    mean_rows = row_sums / count
    variance = square_sums / count - mean_rows * mean_rows
    scale_rows = lax.rsqrt(variance + epsilon) * bn_gain
    normed_here = ((projected - mean_rows) * scale_rows + bn_bias).astype(jnp.bfloat16)
    returned = lax.all_to_all(normed_here, "dp", split_axis=0, concat_axis=0, tiled=True)
    normed = reorder(returned, back_order)
    encoded = jax.nn.relu(normed.astype(jnp.float32) + residual.astype(jnp.float32))
    return encoded.astype(jnp.bfloat16)


ORDER = (0, 1)


def fused_kernel(
    n_dp,
    images,
    positions,
    keys_ref,
    reduce_ref,
    expand_ref,
    weight_ref,
    gain_ref,
    bias_ref,
    shuffle_ref,
    out_ref,
    w,
    w_last,
    red,
    exp,
    relay_w,
    relay_red,
    relay_exp,
    kbuf,
    psend,
    precv,
    rsend,
    rrecv,
    keysv,
    ksend,
    nsend,
    nrecv,
    gain,
    bias,
    places,
    key_sem,
    key_send_sem,
    key_recv_sem,
    local_sem,
    pair_send_sem,
    pair_recv_sem,
    cross_send_sem,
    cross_recv_sem,
    spread_send_sem,
    spread_recv_sem,
    narrow_sem,
    wide_sem,
    back_send_sem,
    back_recv_sem,
):
    me = lax.axis_index("dp")
    f = lax.axis_index("fsdp")
    x, c = f // 2, f % 2
    hub = 2 * x + 1
    peer_hub = 2 * (1 - x) + 1
    peer_even = 2 * (1 - x)
    layers, rows_dev, channels = weight_ref.shape
    half = 2 * rows_dev
    window = kbuf.shape[4]
    pad = window - half
    rows = images * positions
    piece = half // 4
    parts = ((0, 32), (32, 80), (0, 112), (0, 32), (32, 48), (80, 32))
    quarter = lax.rem(me, 4)
    own_lo = pl.multiple_of(x * (channels - window), lane)
    peer_lo = pl.multiple_of((1 - x) * (channels - window), lane)
    base = pl.multiple_of(x * pad + c * rows_dev, 16)
    last_base = pl.multiple_of(f * rows_dev, 16)

    barrier = pltpu.get_barrier_semaphore()

    def partner(k):
        target = me
        for bit in (4, 2, 1):
            if k & bit:
                target = target + bit - 2 * bit * lax.rem(target // bit, 2)
        return target

    far_first = tuple(range(n_dp - 1, -1, -1))

    def greet(dp, fsdp):
        pl.semaphore_signal(
            barrier, inc=1, device_id={"dp": dp, "fsdp": fsdp}, device_id_type=MESH
        )

    @pl.when(c == 1)
    def _():
        for k in far_first:
            target = partner(k)
            greet(target, peer_hub)
            greet(target, 2 * (1 - x))
            if k > 0:
                greet(target, hub)
            greet(target, 2 * x)

    @pl.when(c == 0)
    def _():
        for k in far_first:
            greet(partner(k), hub)
        greet(me, peer_even)
        greet(me, peer_hub)

    keys_local = pltpu.make_async_copy(keys_ref, keysv, key_sem.at[0])
    keys_local.start()
    places_local = pltpu.make_async_copy(shuffle_ref, places, key_sem.at[1])
    places_local.start()
    norm_local = [
        pltpu.make_async_copy(gain_ref, gain, key_sem.at[2]),
        pltpu.make_async_copy(bias_ref, bias, key_sem.at[3]),
    ]

    own_sources = [weight_ref.at[0], weight_ref.at[1], reduce_ref, expand_ref, weight_ref.at[2]]
    full_targets = [w.at[0], w.at[1], red, exp, w_last]

    def shard_of(s):
        return full_targets[s].at[pl.ds(base if s < 2 else last_base, rows_dev), :]

    locals_ = [
        pltpu.make_async_copy(own_sources[s], shard_of(s), local_sem.at[s]) for s in range(5)
    ]

    @pl.when(c == 1)
    def _():
        for copy in locals_ + norm_local:
            copy.start()
        zero_lo = pl.multiple_of((1 - x) * half, 16)
        for l in range(2):
            w[l, pl.ds(zero_lo, pad), :] = jnp.zeros((pad, channels), w.dtype)

    places_local.wait()
    dests = [lax.div(places[i], images) for i in range(images)]
    keys_local.wait()
    for e in range(n_dp):
        chosen = jnp.int32(0)
        for i in range(images):
            chosen = jnp.where(dests[i] == e, i, chosen)
        ksend[e] = keysv[chosen]

    pl.semaphore_wait(barrier, 2 * n_dp + 1 + c * (n_dp - 1))

    def remote(src, dst, send, recv, fsdp, dp=None):
        return pltpu.make_async_remote_copy(
            src_ref=src,
            dst_ref=dst,
            send_sem=send,
            recv_sem=recv,
            device_id={"dp": me if dp is None else dp, "fsdp": fsdp},
            device_id_type=MESH,
        )

    def key_copy(k, side):
        target = partner(k)
        column, lo = ((hub, own_lo), (peer_hub, peer_lo))[side]
        return remote(
            ksend.at[target, :, pl.ds(lo, window)],
            kbuf.at[c, x, me],
            key_send_sem.at[side, k],
            key_recv_sem.at[c, k // 4],
            column,
            target,
        )

    pair = [
        remote(own_sources[s], shard_of(s), pair_send_sem.at[s], pair_recv_sem.at[s], hub)
        for s in range(5)
    ]

    part_sources = [(reduce_ref, expand_ref, weight_ref.at[2])[i] for i in [0, 0, 1, 2, 2, 2]]
    part_relays = [(relay_red, relay_exp, relay_w)[i] for i in [0, 0, 1, 2, 2, 2]]
    part_targets = [(red, exp, w_last)[i] for i in [0, 0, 1, 2, 2, 2]]

    def cross(t):
        at, size = parts[t]
        lo = pl.multiple_of(lax.rem(me, 2) * piece + at, 16)
        return remote(
            part_sources[t].at[pl.ds(lo, size), :],
            part_relays[t].at[pl.ds(at, size), :],
            cross_send_sem.at[t],
            cross_recv_sem.at[t],
            peer_even,
        )

    crosses = [cross(t) for t in range(6)]
    sends_piece = c == quarter // 2

    def key_order():
        return [(k, side) for k in far_first for side in (1, 0)]

    @pl.when(c == 0)
    def _():
        pair[0].start()
        for k, side in key_order():
            key_copy(k, side).start()

    @pl.when(c == 1)
    def _():
        for k, side in key_order():
            if k > 0 or side > 0:
                key_copy(k, side).start()
        pltpu.make_async_copy(
            ksend.at[me, :, pl.ds(own_lo, window)], kbuf.at[1, x, me], key_recv_sem.at[1, 0]
        ).start()

    @pl.when(sends_piece)
    def _():
        for copy in crosses[:-1]:
            copy.start()

    @pl.when(c == 0)
    def _():
        for copy in pair[1:]:
            copy.start()

    def part_copy(t, q, j):
        at, size = parts[t]
        lo = pl.multiple_of((1 - x) * half + q * piece + at, 16)
        return remote(
            part_relays[t].at[pl.ds(at, size), :],
            part_targets[t].at[pl.ds(lo, size), :],
            spread_send_sem.at[t, j],
            spread_recv_sem.at[t, q],
            hub,
            partner(j),
        )

    @pl.when(c == 0)
    def _():
        for t in range(6):
            crosses[t].wait_recv()
            if t == 0:

                @pl.when(quarter < 2)
                def _():
                    for copy in crosses[-1:]:
                        copy.start()

            for j in (3, 2, 1, 0):
                part_copy(t, quarter, j).start()
        for k, side in key_order():
            key_copy(k, side).wait_send()
        for copy in pair:
            copy.wait_send()
        for t in range(6):
            for j in range(4):
                part_copy(t, quarter, j).wait_send()

    def half_start(far):
        near = me // 4
        return 4 * (1 - near if far else near)

    def back_copy(g, k):
        target = partner(k)
        slot = lax.rem(target, 4) + k // 4 * 4
        if g == 1 and k == 0:
            return pltpu.make_async_copy(nsend.at[g, slot], nrecv.at[me], back_recv_sem)
        return remote(
            nsend.at[g, slot],
            nrecv.at[me],
            back_send_sem.at[g, k],
            back_recv_sem,
            2 * x + g,
            target,
        )

    def have(s):
        locals_[s].wait()
        pair[s].wait_recv()

    def have_full(t):
        have(t + 2)
        for p in [p for p, i in enumerate([0, 0, 1, 2, 2, 2]) if i == t]:
            for q in range(4):
                part_copy(p, q, 0).wait_recv()

    @pl.when(c == 1)
    def _():
        narrow = [
            remote(psend.at[j], precv.at[j], narrow_sem.at[0, j], narrow_sem.at[1, j], peer_hub)
            for j in range(4)
        ]
        wide = [
            remote(rsend.at[j], rrecv.at[j], wide_sem.at[0, j], wide_sem.at[1, j], peer_hub)
            for j in range(4)
        ]
        chunks = [(far, g, 2 * far + i) for far in range(2) for i, g in enumerate(ORDER)]
        half_rows = rows // 2
        have(0)
        mines = [None] * 4
        entries = [None] * 4
        for far in range(2):
            for _, g, j in chunks[2 * far : 2 * far + 2]:
                if j == 1:

                    @pl.when(quarter >= 2)
                    def _():
                        for copy in crosses[-1:]:
                            copy.start()

                sources = pl.ds(pl.multiple_of(half_start(far), 4), 4)
                remote(
                    kbuf.at[g, :, sources],
                    kbuf.at[g, :, sources],
                    key_send_sem.at[0, 0],
                    key_recv_sem.at[g, far],
                    hub,
                ).wait_recv()
                entries[j] = (
                    kbuf[g, :, sources]
                    .astype(jnp.float32)
                    .reshape(rows, window)
                    .astype(jnp.bfloat16)
                )
                theirs = jnp.dot(
                    entries[j], w[0, :, pl.ds(peer_lo, window)], preferred_element_type=jnp.float32
                )
                psend[j] = theirs.astype(jnp.bfloat16)
                narrow[j].start()
            own = jnp.dot(
                jnp.concatenate(entries[2 * far : 2 * far + 2], axis=0),
                w[0, :, pl.ds(own_lo, window)],
                preferred_element_type=jnp.float32,
            )
            mines[2 * far], mines[2 * far + 1] = own[:rows], own[rows:]
        have(1)
        for _, g, j in chunks:
            narrow[j].wait_recv()
            full = mines[j] + precv[j].astype(jnp.float32)
            entry = jnp.maximum(full, 0.0).astype(jnp.bfloat16)
            low, high = entry[:half_rows], entry[half_rows:]
            rsend[j] = jnp.dot(
                jnp.where(x == 0, high, low), w[1], preferred_element_type=jnp.float32
            ).astype(jnp.bfloat16)
            wide[j].start()
            entries[j] = jnp.where(x == 0, low, high)
        own = jnp.dot(
            jnp.concatenate(entries, axis=0), w[1], preferred_element_type=jnp.float32
        )
        for j in range(4):
            mines[j] = own[j * half_rows : (j + 1) * half_rows]
        for k, side in key_order():
            if k > 0 or side > 0:
                key_copy(k, side).wait_send()
        have_full(0)
        have_full(1)
        for copy in norm_local:
            copy.wait()
        scaled = [None, None]
        for i, g in enumerate(ORDER):
            settled = []
            for j in (i, i + 2):
                wide[j].wait_recv()
                full = mines[j] + rrecv[j].astype(jnp.float32)
                settled.append(jnp.maximum(full, 0.0).astype(jnp.bfloat16))
            entry = jnp.concatenate(settled, axis=0)
            spots = entry.astype(jnp.float32).reshape(images, positions, channels)
            pooled = (jnp.sum(spots, axis=1) * (1.0 / positions)).astype(jnp.bfloat16)
            squeeze_act = jnp.maximum(
                jnp.dot(pooled, red[...], preferred_element_type=jnp.float32), 0.0
            ).astype(jnp.bfloat16)
            excite = jax.nn.sigmoid(
                lax.dot_general(
                    squeeze_act,
                    exp[...],
                    (((1,), (1,)), ((), ())),
                    preferred_element_type=jnp.float32,
                )
            )
            scaled[g] = (
                (spots * excite[:, None, :]).reshape(rows, channels).astype(jnp.bfloat16)
            )
            if g == ORDER[0]:
                have_full(2)
            projected = jnp.dot(scaled[g], w_last[...], preferred_element_type=jnp.float32)
            mean_rows = jnp.sum(projected, axis=0, keepdims=True) / rows
            squares = jnp.sum(projected * projected, axis=0, keepdims=True) / rows
            scale_rows = lax.rsqrt(squares - mean_rows * mean_rows + epsilon) * gain[
                ...
            ].reshape(1, channels)
            offset = bias[...].reshape(1, channels)
            for far in (1, 0):
                part = projected[far * half_rows : (far + 1) * half_rows]
                normed = (part - mean_rows) * scale_rows + offset
                nsend[g, 4 * far : 4 * far + 4] = normed.reshape(
                    images // 2, positions, channels
                ).astype(jnp.bfloat16)
                for k in (7, 6, 5, 4) if far else (3, 2, 1, 0):
                    back_copy(g, k).start()
        for j in range(4):
            narrow[j].wait_send()
            wide[j].wait_send()

    @pl.when(sends_piece)
    def _():
        for copy in crosses:
            copy.wait_send()

    remote(nrecv, nrecv, back_send_sem.at[0, 0], back_recv_sem, hub).wait_recv()
    for i in range(images):
        out_ref[i] = nrecv[dests[i]]

    @pl.when(c == 1)
    def _():
        for g in range(2):
            for k in range(n_dp):
                if g == 0 or k > 0:
                    back_copy(g, k).wait_send()


def local_fused(n_dp, keys, residual, se_reduce, se_expand, conv_weight, bn_gain, bn_bias, shuffle, unshuffle):
    images, positions, channels = keys.shape
    layers, rows_dev, _ = conv_weight.shape
    units = se_reduce.shape[1]
    rows = images * positions
    half = 2 * rows_dev
    piece = half // 4
    window = -(-half // lane) * lane
    bf16, f32 = jnp.bfloat16, jnp.float32
    vmem = pl.BlockSpec(memory_space=pltpu.VMEM)
    anywhere = pl.BlockSpec(memory_space=pl.ANY)
    dma = pltpu.SemaphoreType.DMA
    normed = pl.pallas_call(
        functools.partial(fused_kernel, n_dp, images, positions),
        out_shape=pltpu.VMEM((images, positions, channels), bf16),
        in_specs=[anywhere] * 7,
        out_specs=vmem,
        scratch_shapes=[
            pltpu.VMEM((2, window, channels), bf16),
            pltpu.VMEM((2 * half, channels), bf16),
            pltpu.VMEM((2 * half, units), bf16),
            pltpu.VMEM((2 * half, units), bf16),
            pltpu.VMEM((piece, channels), bf16),
            pltpu.VMEM((piece, units), bf16),
            pltpu.VMEM((piece, units), bf16),
            pltpu.VMEM((2, 2, images, positions, window), bf16),
            pltpu.VMEM((4, rows, window), bf16),
            pltpu.VMEM((4, rows, window), bf16),
            pltpu.VMEM((4, rows // 2, channels), bf16),
            pltpu.VMEM((4, rows // 2, channels), bf16),
            pltpu.VMEM((images, positions, channels), bf16),
            pltpu.VMEM((n_dp, positions, channels), bf16),
            pltpu.VMEM((2, images, positions, channels), bf16),
            pltpu.VMEM((n_dp, positions, channels), bf16),
            pltpu.VMEM((channels,), f32),
            pltpu.VMEM((channels,), f32),
            pltpu.SMEM((images,), jnp.int32),
            dma((4,)),
            dma((2, n_dp)),
            dma((2, 2)),
            dma((5,)),
            dma((5,)),
            dma((5,)),
            dma((6,)),
            dma((6,)),
            dma((6, 4)),
            dma((6, 4)),
            dma((2, 4)),
            dma((2, 4)),
            dma((2, n_dp)),
            dma,
        ],
        compiler_params=pltpu.CompilerParams(collective_id=0, has_side_effects=True),
        name="fused_encoder",
    )(
        keys,
        se_reduce,
        se_expand,
        conv_weight,
        bn_gain,
        bn_bias,
        shuffle,
    )
    encoded = jax.nn.relu(normed.astype(f32) + residual.astype(f32))
    return encoded.astype(bf16)


def solution(mesh):
    placed = (
        P(("dp", "fsdp"), None, None),
        P(("dp", "fsdp"), None, None),
        P("fsdp", None),
        P("fsdp", None),
        P(None, "fsdp", None),
        P(),
        P(),
        P(("dp", "fsdp")),
        P(("dp", "fsdp")),
    )
    n_dp, n_fsdp = mesh.shape["dp"], mesh.shape["fsdp"]

    def local(keys, *others):
        if n_fsdp == 4 and n_dp == 8 and keys.shape[0] == n_dp:
            return local_fused(n_dp, keys, *others)
        return local_general(keys, *others)

    return jax.shard_map(
        local, mesh=mesh, in_specs=placed, out_specs=P(("dp", "fsdp"), None, None), check_vma=False
    )
```

```python
import functools

import jax
import jax.numpy as jnp
from jax import lax
from jax.experimental import pallas as pl
from jax.experimental.pallas import tpu as pltpu
from jax.sharding import PartitionSpec as P

epsilon = 1e-05
lane = 128
MESH = pl.DeviceIdType.MESH


def project_rows(flat, weight_rows):
    return jnp.dot(
        flat,
        lax.all_gather(weight_rows, "fsdp", axis=0, tiled=True),
        preferred_element_type=jnp.float32,
    )


def reorder(images_block, order):
    images, positions, channels = images_block.shape
    chosen = (order[:, None] == jnp.arange(images)[None, :]).astype(images_block.dtype)
    picked = jnp.dot(
        chosen,
        images_block.reshape(images, positions * channels),
        preferred_element_type=jnp.float32,
    )
    return picked.astype(images_block.dtype).reshape(images_block.shape)


def encode_block(batch_block, reduce_full, expand_full, conv_weight):
    images, positions, channels = batch_block.shape
    layers = conv_weight.shape[0]
    flat = batch_block.reshape(images * positions, channels)
    for layer in range(layers - 1):
        flat = jax.nn.relu(project_rows(flat, conv_weight[layer])).astype(jnp.bfloat16)
    entry = flat.reshape(images, positions, channels)
    pooled = jnp.mean(entry, axis=1, dtype=jnp.float32).astype(jnp.bfloat16)
    squeeze_act = jax.nn.relu(
        jnp.dot(pooled, reduce_full, preferred_element_type=jnp.float32)
    ).astype(jnp.bfloat16)
    excite = jax.nn.sigmoid(
        lax.dot_general(
            squeeze_act, expand_full, (((1,), (1,)), ((), ())), preferred_element_type=jnp.float32
        )
    )
    scaled = (entry * excite[:, None, :]).astype(jnp.bfloat16).reshape(images * positions, channels)
    projected = project_rows(scaled, conv_weight[layers - 1])
    return projected.reshape(images, positions, channels)


def local_general(keys, residual, se_reduce, se_expand, conv_weight, bn_gain, bn_bias, shuffle, unshuffle):
    images, positions, channels = keys.shape
    count = images * positions
    reduce_full, expand_full = (
        lax.all_gather(se_reduce, "fsdp", axis=0, tiled=True),
        lax.all_gather(se_expand, "fsdp", axis=0, tiled=True),
    )
    send_order = jnp.argsort(shuffle)
    back_order = jnp.argsort(send_order)
    outgoing = reorder(keys, send_order)
    arrived = lax.all_to_all(outgoing, "dp", split_axis=0, concat_axis=0, tiled=True)
    projected = encode_block(arrived, reduce_full, expand_full, conv_weight)
    row_sums = jnp.sum(projected, axis=(0, 1))
    square_sums = jnp.sum(projected * projected, axis=(0, 1))
    mean_rows = row_sums / count
    variance = square_sums / count - mean_rows * mean_rows
    scale_rows = lax.rsqrt(variance + epsilon) * bn_gain
    normed_here = ((projected - mean_rows) * scale_rows + bn_bias).astype(jnp.bfloat16)
    returned = lax.all_to_all(normed_here, "dp", split_axis=0, concat_axis=0, tiled=True)
    normed = reorder(returned, back_order)
    encoded = jax.nn.relu(normed.astype(jnp.float32) + residual.astype(jnp.float32))
    return encoded.astype(jnp.bfloat16)


ORDER = (0, 1)


def fused_kernel(
    n_dp,
    images,
    positions,
    keys_ref,
    reduce_ref,
    expand_ref,
    weight_ref,
    gain_ref,
    bias_ref,
    shuffle_ref,
    out_ref,
    w,
    w_last,
    red,
    exp,
    relay_w,
    relay_red,
    relay_exp,
    kbuf,
    psend,
    precv,
    rsend,
    rrecv,
    keysv,
    ksend,
    nsend,
    nrecv,
    gain,
    bias,
    places,
    key_sem,
    key_send_sem,
    key_recv_sem,
    local_sem,
    pair_send_sem,
    pair_recv_sem,
    cross_send_sem,
    cross_recv_sem,
    spread_send_sem,
    spread_recv_sem,
    narrow_sem,
    wide_sem,
    back_send_sem,
    back_recv_sem,
):
    me = lax.axis_index("dp")
    f = lax.axis_index("fsdp")
    x, c = f // 2, f % 2
    hub = 2 * x + 1
    peer_hub = 2 * (1 - x) + 1
    peer_even = 2 * (1 - x)
    layers, rows_dev, channels = weight_ref.shape
    half = 2 * rows_dev
    window = kbuf.shape[4]
    pad = window - half
    rows = images * positions
    piece = half // 4
    parts = ((0, 32), (32, 80), (0, 112), (0, 32), (32, 48), (80, 32))
    quarter = lax.rem(me, 4)
    own_lo = pl.multiple_of(x * (channels - window), lane)
    peer_lo = pl.multiple_of((1 - x) * (channels - window), lane)
    base = pl.multiple_of(x * pad + c * rows_dev, 16)
    last_base = pl.multiple_of(f * rows_dev, 16)

    barrier = pltpu.get_barrier_semaphore()

    def partner(k):
        target = me
        for bit in (4, 2, 1):
            if k & bit:
                target = target + bit - 2 * bit * lax.rem(target // bit, 2)
        return target

    far_first = tuple(range(n_dp - 1, -1, -1))

    def greet(dp, fsdp):
        pl.semaphore_signal(
            barrier, inc=1, device_id={"dp": dp, "fsdp": fsdp}, device_id_type=MESH
        )

    @pl.when(c == 1)
    def _():
        for k in far_first:
            target = partner(k)
            greet(target, peer_hub)
            greet(target, 2 * (1 - x))
            if k > 0:
                greet(target, hub)
            greet(target, 2 * x)

    @pl.when(c == 0)
    def _():
        for k in far_first:
            greet(partner(k), hub)
        greet(me, peer_even)
        greet(me, peer_hub)

    keys_local = pltpu.make_async_copy(keys_ref, keysv, key_sem.at[0])
    keys_local.start()
    places_local = pltpu.make_async_copy(shuffle_ref, places, key_sem.at[1])
    places_local.start()
    norm_local = [
        pltpu.make_async_copy(gain_ref, gain, key_sem.at[2]),
        pltpu.make_async_copy(bias_ref, bias, key_sem.at[3]),
    ]

    own_sources = [weight_ref.at[0], weight_ref.at[1], reduce_ref, expand_ref, weight_ref.at[2]]
    full_targets = [w.at[0], w.at[1], red, exp, w_last]

    def shard_of(s):
        return full_targets[s].at[pl.ds(base if s < 2 else last_base, rows_dev), :]

    locals_ = [
        pltpu.make_async_copy(own_sources[s], shard_of(s), local_sem.at[s]) for s in range(5)
    ]

    @pl.when(c == 1)
    def _():
        for copy in locals_ + norm_local:
            copy.start()
        zero_lo = pl.multiple_of((1 - x) * half, 16)
        for l in range(2):
            w[l, pl.ds(zero_lo, pad), :] = jnp.zeros((pad, channels), w.dtype)

    places_local.wait()
    dests = [lax.div(places[i], images) for i in range(images)]
    keys_local.wait()
    for e in range(n_dp):
        chosen = jnp.int32(0)
        for i in range(images):
            chosen = jnp.where(dests[i] == e, i, chosen)
        ksend[e] = keysv[chosen]

    pl.semaphore_wait(barrier, 2 * n_dp + 1 + c * (n_dp - 1))

    def remote(src, dst, send, recv, fsdp, dp=None):
        return pltpu.make_async_remote_copy(
            src_ref=src,
            dst_ref=dst,
            send_sem=send,
            recv_sem=recv,
            device_id={"dp": me if dp is None else dp, "fsdp": fsdp},
            device_id_type=MESH,
        )

    def key_copy(k, side):
        target = partner(k)
        column, lo = ((hub, own_lo), (peer_hub, peer_lo))[side]
        return remote(
            ksend.at[target, :, pl.ds(lo, window)],
            kbuf.at[c, x, me],
            key_send_sem.at[side, k],
            key_recv_sem.at[c, k // 4],
            column,
            target,
        )

    pair = [
        remote(own_sources[s], shard_of(s), pair_send_sem.at[s], pair_recv_sem.at[s], hub)
        for s in range(5)
    ]

    part_sources = [(reduce_ref, expand_ref, weight_ref.at[2])[i] for i in [0, 0, 1, 2, 2, 2]]
    part_relays = [(relay_red, relay_exp, relay_w)[i] for i in [0, 0, 1, 2, 2, 2]]
    part_targets = [(red, exp, w_last)[i] for i in [0, 0, 1, 2, 2, 2]]

    def cross(t):
        at, size = parts[t]
        lo = pl.multiple_of(lax.rem(me, 2) * piece + at, 16)
        return remote(
            part_sources[t].at[pl.ds(lo, size), :],
            part_relays[t].at[pl.ds(at, size), :],
            cross_send_sem.at[t],
            cross_recv_sem.at[t],
            peer_even,
        )

    crosses = [cross(t) for t in range(6)]
    sends_piece = c == quarter // 2

    def key_order():
        return [(k, side) for k in far_first for side in (1, 0)]

    @pl.when(c == 0)
    def _():
        pair[0].start()
        for k, side in key_order():
            key_copy(k, side).start()

    @pl.when(c == 1)
    def _():
        for k, side in key_order():
            if k > 0 or side > 0:
                key_copy(k, side).start()
        pltpu.make_async_copy(
            ksend.at[me, :, pl.ds(own_lo, window)], kbuf.at[1, x, me], key_recv_sem.at[1, 0]
        ).start()

    @pl.when(sends_piece)
    def _():
        for copy in crosses[:-1]:
            copy.start()

    @pl.when(c == 0)
    def _():
        for copy in pair[1:]:
            copy.start()

    def part_copy(t, q, j):
        at, size = parts[t]
        lo = pl.multiple_of((1 - x) * half + q * piece + at, 16)
        return remote(
            part_relays[t].at[pl.ds(at, size), :],
            part_targets[t].at[pl.ds(lo, size), :],
            spread_send_sem.at[t, j],
            spread_recv_sem.at[t, q],
            hub,
            partner(j),
        )

    @pl.when(c == 0)
    def _():
        for t in range(6):
            crosses[t].wait_recv()
            if t == 0:

                @pl.when(quarter < 2)
                def _():
                    for copy in crosses[-1:]:
                        copy.start()

            for j in (3, 2, 1, 0):
                part_copy(t, quarter, j).start()
        for k, side in key_order():
            key_copy(k, side).wait_send()
        for copy in pair:
            copy.wait_send()
        for t in range(6):
            for j in range(4):
                part_copy(t, quarter, j).wait_send()

    def half_start(far):
        near = me // 4
        return 4 * (1 - near if far else near)

    def back_copy(g, k):
        target = partner(k)
        slot = lax.rem(target, 4) + k // 4 * 4
        if g == 1 and k == 0:
            return pltpu.make_async_copy(nsend.at[g, slot], nrecv.at[me], back_recv_sem)
        return remote(
            nsend.at[g, slot],
            nrecv.at[me],
            back_send_sem.at[g, k],
            back_recv_sem,
            2 * x + g,
            target,
        )

    def have(s):
        locals_[s].wait()
        pair[s].wait_recv()

    def have_full(t):
        have(t + 2)
        for p in [p for p, i in enumerate([0, 0, 1, 2, 2, 2]) if i == t]:
            for q in range(4):
                part_copy(p, q, 0).wait_recv()

    @pl.when(c == 1)
    def _():
        narrow = [
            remote(psend.at[j], precv.at[j], narrow_sem.at[0, j], narrow_sem.at[1, j], peer_hub)
            for j in range(4)
        ]
        wide = [
            remote(rsend.at[j], rrecv.at[j], wide_sem.at[0, j], wide_sem.at[1, j], peer_hub)
            for j in range(4)
        ]
        chunks = [(far, g, 2 * far + i) for far in range(2) for i, g in enumerate(ORDER)]
        half_rows = rows // 2
        have(0)
        mines = [None] * 4
        entries = [None] * 4
        for far in range(2):
            for _, g, j in chunks[2 * far : 2 * far + 2]:
                if j == 1:

                    @pl.when(quarter >= 2)
                    def _():
                        for copy in crosses[-1:]:
                            copy.start()

                sources = pl.ds(pl.multiple_of(half_start(far), 4), 4)
                remote(
                    kbuf.at[g, :, sources],
                    kbuf.at[g, :, sources],
                    key_send_sem.at[0, 0],
                    key_recv_sem.at[g, far],
                    hub,
                ).wait_recv()
                entries[j] = (
                    kbuf[g, :, sources]
                    .astype(jnp.float32)
                    .reshape(rows, window)
                    .astype(jnp.bfloat16)
                )
                theirs = jnp.dot(
                    entries[j], w[0, :, pl.ds(peer_lo, window)], preferred_element_type=jnp.float32
                )
                psend[j] = theirs.astype(jnp.bfloat16)
                narrow[j].start()
            own = jnp.dot(
                jnp.concatenate(entries[2 * far : 2 * far + 2], axis=0),
                w[0, :, pl.ds(own_lo, window)],
                preferred_element_type=jnp.float32,
            )
            mines[2 * far], mines[2 * far + 1] = own[:rows], own[rows:]
        have(1)
        for _, g, j in chunks:
            narrow[j].wait_recv()
            full = mines[j] + precv[j].astype(jnp.float32)
            entry = jnp.maximum(full, 0.0).astype(jnp.bfloat16)
            both = jnp.dot(entry, w[1], preferred_element_type=jnp.float32)
            low, high = both[:half_rows], both[half_rows:]
            rsend[j] = jnp.where(x == 0, high, low).astype(jnp.bfloat16)
            wide[j].start()
            mines[j] = jnp.where(x == 0, low, high)
        for k, side in key_order():
            if k > 0 or side > 0:
                key_copy(k, side).wait_send()
        have_full(0)
        have_full(1)
        for copy in norm_local:
            copy.wait()
        scaled = [None, None]
        for i, g in enumerate(ORDER):
            settled = []
            for j in (i, i + 2):
                wide[j].wait_recv()
                full = mines[j] + rrecv[j].astype(jnp.float32)
                settled.append(jnp.maximum(full, 0.0).astype(jnp.bfloat16))
            entry = jnp.concatenate(settled, axis=0)
            spots = entry.astype(jnp.float32).reshape(images, positions, channels)
            pooled = (jnp.sum(spots, axis=1) * (1.0 / positions)).astype(jnp.bfloat16)
            squeeze_act = jnp.maximum(
                jnp.dot(pooled, red[...], preferred_element_type=jnp.float32), 0.0
            ).astype(jnp.bfloat16)
            excite = jax.nn.sigmoid(
                lax.dot_general(
                    squeeze_act,
                    exp[...],
                    (((1,), (1,)), ((), ())),
                    preferred_element_type=jnp.float32,
                )
            )
            scaled[g] = (
                (spots * excite[:, None, :]).reshape(rows, channels).astype(jnp.bfloat16)
            )
            if g == ORDER[0]:
                have_full(2)
            projected = jnp.dot(scaled[g], w_last[...], preferred_element_type=jnp.float32)
            mean_rows = jnp.sum(projected, axis=0, keepdims=True) / rows
            squares = jnp.sum(projected * projected, axis=0, keepdims=True) / rows
            scale_rows = lax.rsqrt(squares - mean_rows * mean_rows + epsilon) * gain[
                ...
            ].reshape(1, channels)
            normed = (projected - mean_rows) * scale_rows + bias[...].reshape(1, channels)
            nsend[g] = normed.reshape(images, positions, channels).astype(jnp.bfloat16)
            for k in far_first:
                back_copy(g, k).start()
        for j in range(4):
            narrow[j].wait_send()
            wide[j].wait_send()

    @pl.when(sends_piece)
    def _():
        for copy in crosses:
            copy.wait_send()

    remote(nrecv, nrecv, back_send_sem.at[0, 0], back_recv_sem, hub).wait_recv()
    for i in range(images):
        out_ref[i] = nrecv[dests[i]]

    @pl.when(c == 1)
    def _():
        for g in range(2):
            for k in range(n_dp):
                if g == 0 or k > 0:
                    back_copy(g, k).wait_send()


def local_fused(n_dp, keys, residual, se_reduce, se_expand, conv_weight, bn_gain, bn_bias, shuffle, unshuffle):
    images, positions, channels = keys.shape
    layers, rows_dev, _ = conv_weight.shape
    units = se_reduce.shape[1]
    rows = images * positions
    half = 2 * rows_dev
    piece = half // 4
    window = -(-half // lane) * lane
    bf16, f32 = jnp.bfloat16, jnp.float32
    vmem = pl.BlockSpec(memory_space=pltpu.VMEM)
    anywhere = pl.BlockSpec(memory_space=pl.ANY)
    dma = pltpu.SemaphoreType.DMA
    normed = pl.pallas_call(
        functools.partial(fused_kernel, n_dp, images, positions),
        out_shape=pltpu.VMEM((images, positions, channels), bf16),
        in_specs=[anywhere] * 7,
        out_specs=vmem,
        scratch_shapes=[
            pltpu.VMEM((2, window, channels), bf16),
            pltpu.VMEM((2 * half, channels), bf16),
            pltpu.VMEM((2 * half, units), bf16),
            pltpu.VMEM((2 * half, units), bf16),
            pltpu.VMEM((piece, channels), bf16),
            pltpu.VMEM((piece, units), bf16),
            pltpu.VMEM((piece, units), bf16),
            pltpu.VMEM((2, 2, images, positions, window), bf16),
            pltpu.VMEM((4, rows, window), bf16),
            pltpu.VMEM((4, rows, window), bf16),
            pltpu.VMEM((4, rows // 2, channels), bf16),
            pltpu.VMEM((4, rows // 2, channels), bf16),
            pltpu.VMEM((images, positions, channels), bf16),
            pltpu.VMEM((n_dp, positions, channels), bf16),
            pltpu.VMEM((2, images, positions, channels), bf16),
            pltpu.VMEM((n_dp, positions, channels), bf16),
            pltpu.VMEM((channels,), f32),
            pltpu.VMEM((channels,), f32),
            pltpu.SMEM((images,), jnp.int32),
            dma((4,)),
            dma((2, n_dp)),
            dma((2, 2)),
            dma((5,)),
            dma((5,)),
            dma((5,)),
            dma((6,)),
            dma((6,)),
            dma((6, 4)),
            dma((6, 4)),
            dma((2, 4)),
            dma((2, 4)),
            dma((2, n_dp)),
            dma,
        ],
        compiler_params=pltpu.CompilerParams(collective_id=0, has_side_effects=True),
        name="fused_encoder",
    )(
        keys,
        se_reduce,
        se_expand,
        conv_weight,
        bn_gain,
        bn_bias,
        shuffle,
    )
    encoded = jax.nn.relu(normed.astype(f32) + residual.astype(f32))
    return encoded.astype(bf16)


def solution(mesh):
    placed = (
        P(("dp", "fsdp"), None, None),
        P(("dp", "fsdp"), None, None),
        P("fsdp", None),
        P("fsdp", None),
        P(None, "fsdp", None),
        P(),
        P(),
        P(("dp", "fsdp")),
        P(("dp", "fsdp")),
    )
    n_dp, n_fsdp = mesh.shape["dp"], mesh.shape["fsdp"]

    def local(keys, *others):
        if n_fsdp == 4 and n_dp == 8 and keys.shape[0] == n_dp:
            return local_fused(n_dp, keys, *others)
        return local_general(keys, *others)

    return jax.shard_map(
        local, mesh=mesh, in_specs=placed, out_specs=P(("dp", "fsdp"), None, None), check_vma=False
    )
```
